256 devices in a mesh: days: 4 (over y), space: 64 (over z, x, core).
Axes of the slice: x: 4, y: 4, z: 8, core: 2. Of those that a mesh axis runs over, the one named last changes fastest.
Arguments:
- fields: bfloat16 [640, 256, 1440], P('days', 'space')
- month_label: int32 [640], P('days'), may hold values from 0 to 11, as said below
- row_index: int32 [256], P('space'), may hold values from 0 to 255
- area_table: float32 [256], replicated, may hold values from 0.05 to 1
- basis: bfloat16 [64, 256, 1440], P(None, 'space'), may hold values from -6 to 6
Outputs:
- eofs: float32 [64, 256, 1440], P(None, 'space')
- pcs: float32 [640, 64], P('days')
The draws below stay inside these ranges and needn't reach their ends.
Inputs may be any that keep to these rules, and one draw needn't show every extreme that they name: `month_label`: each day's label differs from floor(12 * day / 640) by at most one; the first day with a given value of floor(12 * day / 640) carries exactly that value; every month labels at least one day.
All inputs are finite; a program needn't handle non-finite values.
Results may differ from the reference program's by a relative error of at most 0.0003.
Values sent between devices are 32-bit elements; how exact they have to be, the bound alone decides.
No kernel may reach another device: no remote copies, remote signals or barrier semaphores. Data moves between devices by JAX's collectives and lax.ppermute only.
A program may use at most 64 MiB of HBM per device.

```python
import math
import jax
import jax.numpy as jnp
from jax import lax

LON = 1440
MODES = 64
ITERS = 2
LAT_DEV = 4
LAT = 256
DAYS = 640
N_SPACE = 64


def month_series(key):
    day = jnp.arange(DAYS, dtype=jnp.int32)
    base = day * 12 // DAYS
    first = base != (day - 1) * 12 // DAYS
    jitter = jax.random.randint(jax.random.fold_in(key, 7), (DAYS,), -1, 2)
    return jnp.where(first, base, jnp.clip(base + jitter, 0, 11)).astype(jnp.int32)


def draw_month_label(key, part):
    return month_series(key)


def draw_fields(key, part):
    labels = month_series(key)
    season = jax.random.normal(jax.random.fold_in(key, 11), (12, LAT, LON), jnp.float32)
    noise = jax.random.normal(jax.random.fold_in(key, 13), (DAYS, LAT, LON), jnp.float32)
    values = 2.0 * season[labels] + noise
    return values.astype(jnp.bfloat16)


def touch_ends(entries, rng, low, top_value):
    dims = entries.shape
    place = [jax.random.randint(jax.random.fold_in(rng, axis), (), 0, dims[axis]) for axis in range(len(dims))]
    entries = entries.at[tuple(place)].set(low)
    longest = dims.index(max(dims))
    place[longest] = (place[longest] + 1) % dims[longest]
    return entries.at[tuple(place)].set(top_value)


def block_scale(rng, extent, shards, smallest, top_value):
    gain, own = 1.0, jax.random.fold_in(rng, 6)
    for dim, shards_of in shards:
        steps = jnp.exp(jax.random.uniform(jax.random.fold_in(own, dim), (shards_of,), jnp.float32, smallest / len(shards), top_value / len(shards)))
        gain = gain * jnp.repeat(steps, extent[dim] // shards_of).reshape([-1 if axis == dim else 1 for axis in range(len(extent))])
    return gain


def scatter_about(own_key, dims, deviation, bound, cuts=(), kind=jnp.bfloat16):
    values = jax.random.normal(own_key, dims, jnp.float32) * deviation
    if len(cuts) > 0:
        values = block_scale(own_key, dims, cuts, -0.22, 0.18) * values
    return jnp.clip(values, min=-bound, max=bound).astype(kind)


def setup_inputs(seed: int = 0) -> dict:
    seeds = jax.random.split(jax.random.key(seed), 6)
    fields = draw_fields(jax.random.fold_in(seeds[5], 71), 0)
    month_label = draw_month_label(jax.random.fold_in(seeds[5], 71), 0)
    row_index = touch_ends(jax.random.randint(seeds[2], (LAT,), 0, LAT), jax.random.fold_in(seeds[2], 1), 0, LAT - 1).astype(jnp.int32)
    area_table = jnp.clip(jnp.exp(jax.random.uniform(seeds[3], (LAT,), jnp.float32, math.log(0.05), math.log(1.0))), 0.05, 1.0)
    basis = scatter_about(seeds[4], (MODES, LAT, LON), 1.0, 6.0, ((1, 64),))
    return dict(fields=fields, month_label=month_label, row_index=row_index, area_table=area_table, basis=basis)


HIGH = lax.Precision.HIGHEST

def reference(fields, month_label, row_index, area_table, basis):
    months = jnp.arange(12, dtype=jnp.int32)
    onehot = (month_label[None, :] == months[:, None]).astype(jnp.float32)
    counts = lax.optimization_barrier(jnp.sum(onehot, axis=1))

    def block_fields(index):
        return lax.dynamic_slice_in_dim(fields, (index * LAT_DEV).astype(jnp.int32), LAT_DEV, 1).astype(jnp.float32)

    def add_sums(index):
        return jnp.einsum('md,dlc->mlc', onehot, block_fields(index), precision=HIGH)
    sums = lax.map(add_sums, jnp.arange(N_SPACE, dtype=jnp.int32))
    climate = sums / counts[None, :, None, None]
    scale = jnp.sqrt(area_table[row_index])

    def anomaly(index):
        seasonal = jnp.einsum('md,mlc->dlc', onehot, climate[index], precision=HIGH)
        rows = lax.dynamic_slice_in_dim(scale, (index * LAT_DEV).astype(jnp.int32), LAT_DEV, 0)
        return (block_fields(index) - seasonal) * rows[None, :, None]

    def project(patterns):

        def step(total, index):
            piece = lax.dynamic_slice_in_dim(patterns, (index * LAT_DEV).astype(jnp.int32), LAT_DEV, 1)
            return (total + jnp.einsum('dlc,klc->dk', anomaly(index), piece, precision=HIGH), None)
        start = jnp.zeros((DAYS, MODES), jnp.float32)
        total, _ = lax.scan(step, start, jnp.arange(N_SPACE, dtype=jnp.int32))
        return total
    pcs = project(basis.astype(jnp.float32))
    for step_count in range(ITERS):

        def cover_block(index):
            return jnp.einsum('dk,dlc->klc', pcs, anomaly(index), precision=HIGH) / DAYS
        blocks = lax.map(cover_block, jnp.arange(N_SPACE, dtype=jnp.int32))
        cover = jnp.moveaxis(blocks, 0, 1).reshape(MODES, LAT * LON)
        gram = jnp.dot(cover, cover.T, precision=HIGH)
        lower = jnp.linalg.cholesky(gram)
        solved = lax.linalg.triangular_solve(lower, cover, left_side=True, lower=True)
        eofs = solved.reshape(MODES, LAT, LON)
        pcs = project(eofs)
    return (eofs, pcs)
```

```python
import jax
import jax.numpy as jnp
from jax import lax
from jax.sharding import PartitionSpec as P

MONTHS = 12
LANES = 128
SIDE = 128
HIGH = lax.Precision.HIGHEST


def to_each(shard, axis):
    devices = lax.axis_size(axis)
    return lax.all_to_all(
        jnp.broadcast_to(shard[None], (devices, *shard.shape)), axis, 0, 0, tiled=True
    )


def summed(tiles, axis):
    return jnp.sum(lax.all_to_all(tiles, axis, 0, 0, tiled=True), axis=0)


def total_everywhere(rows):
    days, space = lax.axis_size("days"), lax.axis_size("space")
    count = rows.shape[0]
    rows = jnp.pad(rows, ((0, -count % (days * space)), (0, 0)))
    part = summed(rows.reshape(days, -1, LANES), "days")
    own = summed(part.reshape(space, 1, -1), "space")
    part = to_each(own, "space").reshape(-1, LANES)
    return to_each(part, "days").reshape(-1, LANES)[:count]


def dot(a, b, dims):
    return lax.dot_general(
        a, b, (dims, ((), ())), precision=HIGH, preferred_element_type=jnp.float32
    )


def pair_blocks(weighted):
    blocks = [weighted[at : at + SIDE] for at in range(0, weighted.shape[0], SIDE)]
    n = len(blocks)
    ahead = n // 2 + 1
    return n, [
        dot(blocks[i], blocks[(i + j) % n], ((1,), (1,))) for i in range(n) for j in range(ahead)
    ]


def whole_of(blocks, n):
    ahead = n // 2 + 1
    grid = [[None] * n for _ in range(n)]
    for i in range(n):
        for j in range(ahead):
            k = (i + j) % n
            block = blocks[i * ahead + j]
            grid[i][k] = block
            if j:
                grid[k][i] = block.T
    return jnp.concatenate([jnp.concatenate(line, axis=1) for line in grid], axis=0)


def inverse_of(lower):
    return lax.linalg.triangular_solve(
        lower, jnp.eye(lower.shape[0], dtype=lower.dtype), left_side=True, lower=True
    )


def local(fields, month_label, row_index, area_table, basis):
    days, lat, lon = fields.shape
    groups = lax.axis_size("days")
    me = lax.axis_index("days")
    wide = -(-(lon + 1) // LANES) * LANES
    modes = basis.shape[0]
    days_total = days * groups

    label = jnp.broadcast_to(month_label.astype(jnp.float32)[None, :, None], (lat, days, 1))
    rows = jnp.concatenate(
        [jnp.swapaxes(fields, 0, 1).astype(jnp.float32), label], axis=2
    )
    rows = jnp.pad(rows, ((0, 0), (0, 0), (0, wide - lon - 1)))
    rows = lax.all_to_all(rows, "days", 0, 0, tiled=True).reshape(days_total, wide)

    months = jnp.arange(MONTHS, dtype=jnp.float32)
    onehot = (rows[:, lon][None, :] == months[:, None]).astype(jnp.float32)
    own = jnp.where(jnp.arange(wide) < lon, rows, 0.0)
    sums = dot(onehot, own, ((1,), (0,)))
    climate = sums / jnp.sum(onehot, axis=1)[:, None]
    seasonal = dot(onehot, climate, ((0,), (0,)))
    table_row = lax.dynamic_index_in_dim(row_index, me, keepdims=False)
    area = jnp.sum(jnp.where(jnp.arange(area_table.shape[0]) == table_row, area_table, 0.0))
    weighted = (own - seasonal) * jnp.sqrt(area)

    start = lax.dynamic_index_in_dim(basis, me, axis=1, keepdims=False).astype(jnp.float32)
    start = jnp.pad(start, ((0, 0), (0, wide - lon)))
    start_pcs = dot(start, weighted, ((1,), (1,)))
    n, blocks = pair_blocks(weighted)
    pieces = blocks + [start_pcs[:, at : at + SIDE] for at in range(0, days_total, SIDE)]
    rows = total_everywhere(jnp.concatenate(pieces, axis=0))

    count = len(blocks)
    blocks = [rows[i * SIDE : (i + 1) * SIDE] for i in range(count)]
    rest = rows[count * SIDE :].reshape(n, modes, SIDE)
    pcs = jnp.moveaxis(rest, 0, 1).reshape(modes, days_total)
    products = whole_of(blocks, n) / days_total

    raw = dot(pcs, products, ((1,), (0,)))
    raw_cover = dot(raw, weighted, ((1,), (0,))) / days_total
    cover = to_each(raw_cover[:, :lon], "days")

    first = inverse_of(jnp.linalg.cholesky(dot(pcs, raw, ((1,), (1,))) / days_total))
    pcs = dot(first, raw, ((1,), (0,)))
    raw = dot(pcs, products, ((1,), (0,)))
    second = inverse_of(jnp.linalg.cholesky(dot(pcs, raw, ((1,), (1,))) / days_total))
    both = dot(second, first, ((1,), (0,)))
    eofs = jnp.einsum("kj,ljc->klc", both, cover, precision=HIGH)
    mine = lax.dynamic_slice_in_dim(raw, me * days, days, axis=1)
    return (eofs, dot(mine, second, ((0,), (1,))))


def solution(mesh):
    placed = (P("days", "space", None), P("days"), P("space"), P(), P(None, "space", None))
    return jax.shard_map(
        local,
        mesh=mesh,
        in_specs=placed,
        out_specs=(P(None, "space", None), P("days", None)),
        check_vma=False,
    )
```

```python
import functools

import jax
import jax.numpy as jnp
from jax import lax
from jax.experimental import pallas as pl
from jax.experimental.pallas import tpu as pltpu
from jax.sharding import Mesh, PartitionSpec as P

MONTHS = 12
LANES = 128
SIDE = 128
HIGH = lax.Precision.HIGHEST
F32 = jnp.float32
BF16 = jnp.bfloat16
INTERPRET = False
SPACE = ("z", "x", "core")
STAGES = ("core", ("days", "x"), "z")


def to_each(shard, axis):
    devices = lax.axis_size(axis)
    return lax.all_to_all(
        jnp.broadcast_to(shard[None], (devices, *shard.shape)), axis, 0, 0, tiled=True
    )


def total_everywhere(rows):
    for axis in STAGES:
        devices = lax.axis_size(axis)
        share = rows.shape[0] // devices
        shape = (devices, 1, share * LANES) if share % 8 else (devices, share, LANES)
        tiles = lax.all_to_all(rows.reshape(shape), axis, 0, 0, tiled=True)
        rows = jnp.sum(tiles, axis=0).reshape(share, LANES)
    for axis in STAGES[::-1]:
        flat = rows.reshape(1, -1) if rows.shape[0] % 8 else rows
        rows = to_each(flat, axis).reshape(-1, LANES)
    return rows


def dot(a, b, dims, precision=HIGH):
    return lax.dot_general(a, b, (dims, ((), ())), precision=precision, preferred_element_type=F32)


def one_pass(a, b, dims):
    return dot(a, b, dims, lax.Precision.DEFAULT)


NT = ((1,), (1,))
NN = ((1,), (0,))


def split(x):
    high = x.astype(BF16)
    return high, (x - high.astype(F32)).astype(BF16)


def runs(first, count, n):
    head = min(count, n - first)
    found = [(first, 0, head)]
    if head < count:
        found.append((0, head, count - head))
    return found


def products_kernel(lon, rows_ref, base_ref, scale_ref, out_ref, high_ref, low_ref):
    days, wide = rows_ref.shape
    modes = base_ref.shape[0]
    n = days // SIDE
    ahead = n // 2 + 1
    at_label = lon // LANES * LANES
    label = rows_ref[:, at_label : at_label + LANES][:, lon - at_label : lon - at_label + 1]
    lane = lax.broadcasted_iota(jnp.int32, (days, LANES), 1)
    thrice = ((lane % 16).astype(F32) == label) & (lane < 48)
    thrice = jnp.where(thrice, 1.0, 0.0)
    hot = jnp.transpose(thrice)[:16]
    counts = jnp.sum(hot, axis=1, keepdims=True)
    sums = one_pass(hot.astype(BF16), rows_ref[...].astype(BF16), NN)
    climate = sums / jnp.maximum(counts, 1.0)
    first, rest = split(climate)
    rest = climate - first.astype(F32)
    second = rest.astype(BF16)
    third = (rest - second.astype(F32)).astype(BF16)
    terms = jnp.concatenate(
        [first.astype(F32), second.astype(F32), third.astype(F32), jnp.zeros((LANES - 48, wide), F32)]
    ).astype(BF16)
    inside = lax.broadcasted_iota(jnp.int32, (SIDE, wide), 1) < lon
    scale = scale_ref[0, 0]
    for i in range(n):
        part = slice(i * SIDE, (i + 1) * SIDE)
        seasonal = one_pass(thrice[part].astype(BF16), terms, NN)
        weighted = jnp.where(inside, (rows_ref[part] - seasonal) * scale, 0.0)
        high, low = split(weighted)
        high_ref[part] = high
        low_ref[part] = low
    for i in range(n):
        part = slice(i * SIDE, (i + 1) * SIDE)
        for block, offset, length in runs(i, ahead, n):
            other = slice(block * SIDE, (block + length) * SIDE)
            product = one_pass(high_ref[part], high_ref[other], NT)
            product += one_pass(high_ref[part], low_ref[other], NT)
            product += one_pass(low_ref[part], high_ref[other], NT)
            for j in range(length):
                at = (i * ahead + offset + j) * SIDE
                out_ref[at : at + SIDE] = product[:, j * SIDE : (j + 1) * SIDE]
    pcs = one_pass(base_ref[...], high_ref[...], NT) + one_pass(base_ref[...], low_ref[...], NT)
    at = n * ahead * SIDE
    for i in range(n):
        out_ref[at : at + modes] = pcs[:, i * SIDE : (i + 1) * SIDE]
        at += modes
    if at < out_ref.shape[0]:
        out_ref[at:] = jnp.zeros((out_ref.shape[0] - at, LANES), F32)


def cover_kernel(rows_ref, high_ref, low_ref, products_ref, pcs_ref, raw_ref, cover_ref):
    modes, days = pcs_ref.shape
    n = days // SIDE
    ahead = n // 2 + 1
    for i in range(n):
        for j in range(ahead):
            k = (i + j) % n
            at = (i * ahead + j) * SIDE
            block = rows_ref[at : at + SIDE] * (1.0 / days)
            products_ref[i * SIDE : (i + 1) * SIDE, k * SIDE : (k + 1) * SIDE] = block
            if j:
                products_ref[k * SIDE : (k + 1) * SIDE, i * SIDE : (i + 1) * SIDE] = block.T
    at = n * ahead * SIDE
    for i in range(n):
        pcs_ref[:, i * SIDE : (i + 1) * SIDE] = rows_ref[at : at + modes]
        at += modes
    raw = dot(pcs_ref[...], products_ref[...], NN)
    raw_ref[...] = raw
    high, low = split(raw * (1.0 / days))
    both = jnp.concatenate([high, low], axis=0)
    by_high = one_pass(both, high_ref[...], NN)
    by_low = one_pass(high, low_ref[...], NN)
    cover = by_high[:modes] + by_high[modes:] + by_low
    cover_ref[...] = cover[:, : cover_ref.shape[1]]


def inverse_factor(gram, modes):
    row = lax.broadcasted_iota(jnp.int32, gram.shape, 0)
    lane = lax.broadcasted_iota(jnp.int32, gram.shape, 1)
    whole = jnp.where(lane < modes, jnp.where(row == lane, 1.0, 0.0), gram)
    blocks = [whole[at : at + 8] for at in range(0, modes, 8)]
    sub = lax.broadcasted_iota(jnp.int32, (8, gram.shape[1]), 0)
    for j in range(modes):
        own, at = divmod(j, 8)
        pivot_row = blocks[own][at : at + 1]
        scaled = pivot_row / pivot_row[:, modes + j : modes + j + 1]
        for b in range(own, modes // 8):
            if b == own and at == 7:
                continue
            column = blocks[b][:, modes + j : modes + j + 1]
            step = column * scaled
            if b == own:
                step = jnp.where(sub > at, step, 0.0)
            blocks[b] = blocks[b] - step
    whole = jnp.concatenate(blocks, axis=0)
    pivots = jnp.sum(jnp.where(lane == row + modes, whole, 0.0), axis=1, keepdims=True)
    return jnp.where(lane < modes, whole / jnp.sqrt(pivots), 0.0)


def chain_kernel(products_ref, pcs_ref, raw_ref, both_ref, last_ref):
    modes, days = pcs_ref.shape
    nothing = jnp.zeros((modes, days), F32)
    raw = raw_ref[...]
    gram = dot(pcs_ref[...], jnp.concatenate([nothing, raw]), NT) * (1.0 / days)
    first = inverse_factor(gram, modes)
    pcs = dot(first, jnp.concatenate([raw, nothing]), NN)
    raw = dot(pcs, products_ref[...], NN)
    gram = dot(pcs, jnp.concatenate([nothing, raw]), NT) * (1.0 / days)
    second = inverse_factor(gram, modes)
    last_ref[...] = dot(second, jnp.concatenate([raw, nothing]), NN)
    both_ref[...] = dot(second, jnp.concatenate([first, jnp.zeros_like(first)]), NN)


def call(kernel, shapes, *arrays, flops, spaces=None):
    whole = pl.BlockSpec(memory_space=pltpu.VMEM)
    size = sum(a.size * a.dtype.itemsize for a in arrays)
    size += sum(a.size * a.dtype.itemsize for a in shapes)
    return pl.pallas_call(
        kernel,
        out_shape=shapes,
        in_specs=spaces or [whole] * len(arrays),
        out_specs=[whole] * len(shapes),
        cost_estimate=pl.CostEstimate(flops=flops, bytes_accessed=size, transcendentals=0),
        compiler_params=pltpu.CompilerParams(vmem_limit_bytes=40 * 2**20),
        interpret=INTERPRET,
    )(*arrays)


def local(fields, month_label, row_index, area_table, basis):
    days, lat, lon = fields.shape
    groups = lax.axis_size("days")
    me = lax.axis_index("days")
    wide = -(-(lon + 1) // LANES) * LANES
    modes = basis.shape[0]
    total = days * groups
    n = total // SIDE
    shape = jax.ShapeDtypeStruct

    label = month_label.astype(F32)[None, :, None]
    rows = jnp.pad(jnp.swapaxes(fields, 0, 1).astype(F32), ((0, 0), (0, 0), (0, wide - lon)))
    rows = jnp.where(lax.broadcasted_iota(jnp.int32, rows.shape, 2) == lon, label, rows)
    rows = lax.all_to_all(rows, "days", 0, 0, tiled=True).reshape(total, wide)

    table_row = lax.dynamic_index_in_dim(row_index, me, keepdims=False)
    area = jnp.sum(jnp.where(jnp.arange(area_table.shape[0]) == table_row, area_table, 0.0))
    start = lax.dynamic_index_in_dim(basis, me, axis=1, keepdims=False)
    start = jnp.pad(start, ((0, 0), (0, wide - lon)))

    count = n * (n // 2 + 1) * SIDE + n * modes
    devices = groups * lax.axis_size(SPACE)
    count += -count % devices
    vmem = pl.BlockSpec(memory_space=pltpu.VMEM)
    pieces, high, low = call(
        functools.partial(products_kernel, lon),
        [shape((count, LANES), F32), shape((total, wide), BF16), shape((total, wide), BF16)],
        rows, start, jnp.sqrt(area).reshape(1, 1),
        flops=2 * 3 * total * (total + modes) * wide,
        spaces=[vmem, vmem, pl.BlockSpec(memory_space=pltpu.SMEM)],
    )
    pieces = total_everywhere(pieces)
    products, pcs, raw, cover = call(
        cover_kernel,
        [shape((total, total), F32), shape((modes, total), F32), shape((modes, total), F32),
         shape((modes, lon), F32)],
        pieces, high, low,
        flops=2 * 3 * modes * total * (total + wide),
    )
    cover = to_each(cover, "days")
    both, last = call(
        chain_kernel,
        [shape((modes, 2 * modes), F32), shape((modes, total), F32)],
        products, pcs, raw,
        flops=2 * 6 * modes * total * (total + 8 * modes),
    )
    eofs = jnp.einsum("kj,ljc->klc", both[:, :modes], cover, precision=HIGH)
    return (eofs, lax.dynamic_slice_in_dim(last, me * days, days, axis=1).T)


def solution(mesh):
    space = mesh.shape["space"]
    cores = 2
    around = 4 if space % 8 == 0 else 1
    parts = Mesh(
        mesh.devices.reshape(mesh.shape["days"], space // around // cores, around, cores),
        ("days", *SPACE),
    )
    placed = (
        P("days", SPACE, None), P("days"), P(SPACE), P(), P(None, SPACE, None),
    )
    return jax.shard_map(
        local,
        mesh=parts,
        in_specs=placed,
        out_specs=(P(None, SPACE, None), P("days", None)),
        check_vma=False,
    )
```

```python
import functools

import jax
import jax.numpy as jnp
from jax import lax
from jax.experimental import pallas as pl
from jax.experimental.pallas import tpu as pltpu
from jax.sharding import Mesh, PartitionSpec as P

LANES = 128
SIDE = 128
HIGH = lax.Precision.HIGHEST
F32 = jnp.float32
BF16 = jnp.bfloat16
INTERPRET = False
SPACE = ("z", "x", "core")
STAGES = ("core", ("days", "x"))
ALONG = "z"


def to_each(shard, axis):
    devices = lax.axis_size(axis)
    return lax.all_to_all(
        jnp.broadcast_to(shard[None], (devices, *shard.shape)), axis, 0, 0, tiled=True
    )


def total_everywhere(rows):
    for axis in STAGES:
        devices = lax.axis_size(axis)
        share = rows.shape[0] // devices
        shape = (devices, 1, share * LANES) if share % 8 else (devices, share, LANES)
        tiles = lax.all_to_all(rows.reshape(shape), axis, 0, 0, tiled=True)
        rows = jnp.sum(tiles, axis=0).reshape(share, LANES)
    rows = jnp.sum(to_each(rows, ALONG), axis=0)
    for axis in STAGES[::-1]:
        flat = rows.reshape(1, -1) if rows.shape[0] % 8 else rows
        rows = to_each(flat, axis).reshape(-1, LANES)
    return rows


def dot(a, b, dims, precision=HIGH):
    return lax.dot_general(a, b, (dims, ((), ())), precision=precision, preferred_element_type=F32)


def one_pass(a, b, dims):
    return dot(a, b, dims, lax.Precision.DEFAULT)


NT = ((1,), (1,))
NN = ((1,), (0,))


def split(x):
    high = x.astype(BF16)
    return high, (x - high.astype(F32)).astype(BF16)


def lower_blocks(n):
    return [(r, c) for c in range(n) for r in range(c, n)]


def products_kernel(lon, rows_ref, base_ref, table_ref, where_ref, out_ref, high_ref, low_ref):
    days, wide = rows_ref.shape
    modes = base_ref.shape[0]
    n = days // SIDE
    at_label = lon // LANES * LANES
    label = rows_ref[:, at_label : at_label + LANES][:, lon - at_label : lon - at_label + 1]
    lane = lax.broadcasted_iota(jnp.int32, (days, LANES), 1)
    thrice = ((lane % 16).astype(F32) == label) & (lane < 48)
    thrice = jnp.where(thrice, 1.0, 0.0)
    hot = jnp.transpose(thrice)[:16]
    counts = jnp.sum(hot, axis=1, keepdims=True)
    sums = one_pass(hot.astype(BF16), rows_ref[...].astype(BF16), NN)
    climate = sums / jnp.maximum(counts, 1.0)
    first = climate.astype(BF16)
    rest = climate - first.astype(F32)
    second = rest.astype(BF16)
    third = (rest - second.astype(F32)).astype(BF16)
    terms = jnp.concatenate(
        [first.astype(F32), second.astype(F32), third.astype(F32), jnp.zeros((LANES - 48, wide), F32)]
    ).astype(BF16)
    inside = lax.broadcasted_iota(jnp.int32, (SIDE, wide), 1) < lon
    entry = lax.broadcasted_iota(jnp.int32, table_ref.shape, 1)
    own = jnp.where(entry == where_ref[where_ref.shape[0] - 1], table_ref[...], 0.0)
    scale = jnp.sqrt(jnp.sum(own, axis=1, keepdims=True))
    for i in range(n):
        part = slice(i * SIDE, (i + 1) * SIDE)
        seasonal = one_pass(thrice[part].astype(BF16), terms, NN)
        weighted = jnp.where(inside, (rows_ref[part] - seasonal) * scale, 0.0)
        high, low = split(weighted)
        high_ref[part] = high
        low_ref[part] = low
    high_ref[days:] = base_ref[...]
    low_ref[days:] = jnp.zeros((modes, wide), BF16)
    order = lower_blocks(n)
    for c in range(0, n, 2):
        group = slice(c * SIDE, min(c + 2, n) * SIDE)
        below = slice(c * SIDE, days + modes)
        product = one_pass(high_ref[below], high_ref[group], NT)
        product += one_pass(high_ref[below], low_ref[group], NT)
        product += one_pass(low_ref[below], high_ref[group], NT)
        for k in range(c, min(c + 2, n)):
            lanes = slice((k - c) * SIDE, (k - c + 1) * SIDE)
            for r in range(k, n):
                at = order.index((r, k)) * SIDE
                out_ref[at : at + SIDE] = product[(r - c) * SIDE : (r - c + 1) * SIDE, lanes]
            at = len(order) * SIDE + k * modes
            out_ref[at : at + modes] = product[days - c * SIDE :, lanes]
    at = len(order) * SIDE + n * modes
    if at < out_ref.shape[0]:
        out_ref[at:] = jnp.zeros((out_ref.shape[0] - at, LANES), F32)


def cover_kernel(rows_ref, high_ref, low_ref, products_ref, pcs_ref, raw_ref, cover_ref):
    modes, days = pcs_ref.shape
    n = days // SIDE
    order = lower_blocks(n)
    for at, (r, c) in enumerate(order):
        block = rows_ref[at * SIDE : (at + 1) * SIDE] * (1.0 / days)
        rows, lanes = slice(r * SIDE, (r + 1) * SIDE), slice(c * SIDE, (c + 1) * SIDE)
        products_ref[rows, lanes] = block
        if r > c:
            products_ref[lanes, rows] = block.T
    at = len(order) * SIDE
    for i in range(n):
        pcs_ref[:, i * SIDE : (i + 1) * SIDE] = rows_ref[at : at + modes]
        at += modes
    raw = dot(pcs_ref[...], products_ref[...], NN)
    raw_ref[...] = raw
    high, low = split(raw * (1.0 / days))
    both = jnp.concatenate([high, low], axis=0)
    by_high = one_pass(both, high_ref[:days], NN)
    by_low = one_pass(high, low_ref[:days], NN)
    cover = by_high[:modes] + by_high[modes:] + by_low
    cover_ref[...] = cover[:, : cover_ref.shape[1]]


def inverse_factor(gram, modes):
    row = lax.broadcasted_iota(jnp.int32, gram.shape, 0)
    lane = lax.broadcasted_iota(jnp.int32, gram.shape, 1)
    whole = jnp.where(lane < modes, jnp.where(row == lane, 1.0, 0.0), gram)
    blocks = [whole[at : at + 8] for at in range(0, modes, 8)]
    sub = lax.broadcasted_iota(jnp.int32, (8, gram.shape[1]), 0)
    for j in range(modes):
        own, at = divmod(j, 8)
        pivot_row = blocks[own][at : at + 1]
        scaled = pivot_row / pivot_row[:, modes + j : modes + j + 1]
        for b in range(own, modes // 8):
            if b == own and at == 7:
                continue
            column = blocks[b][:, modes + j : modes + j + 1]
            step = column * scaled
            if b == own:
                step = jnp.where(sub > at, step, 0.0)
            blocks[b] = blocks[b] - step
    whole = jnp.concatenate(blocks, axis=0)
    pivots = jnp.sum(jnp.where(lane == row + modes, whole, 0.0), axis=1, keepdims=True)
    return jnp.where(lane < modes, whole / jnp.sqrt(pivots), 0.0)


def chain_kernel(products_ref, pcs_ref, raw_ref, both_ref, last_ref):
    modes, days = pcs_ref.shape
    nothing = jnp.zeros((modes, days), F32)
    raw = raw_ref[...]
    gram = dot(pcs_ref[...], jnp.concatenate([nothing, raw]), NT) * (1.0 / days)
    first = inverse_factor(gram, modes)
    pcs = dot(first, jnp.concatenate([raw, nothing]), NN)
    raw = dot(pcs, products_ref[...], NN)
    gram = dot(pcs, jnp.concatenate([nothing, raw]), NT) * (1.0 / days)
    second = inverse_factor(gram, modes)
    last_ref[...] = dot(second, jnp.concatenate([raw, nothing]), NN)
    both_ref[...] = dot(second, jnp.concatenate([first, jnp.zeros_like(first)]), NN)


def patterns_kernel(both_ref, own_ref, before_ref, after_ref, across_ref, where_ref, out_ref):
    modes, lat, lon = out_ref.shape
    me = where_ref[0]
    high, low = split(both_ref[:, :modes])
    stacked = jnp.concatenate([high, low], axis=0)
    for row in range(lat):
        ahead = lax.rem(row - me + lat, lat)
        cover = jnp.where(
            ahead == 0,
            own_ref[...],
            jnp.where(ahead == 1, after_ref[...], jnp.where(ahead == 2, across_ref[...], before_ref[...])),
        )
        cover_high, cover_low = split(cover)
        by_high = one_pass(stacked, cover_high, NN)
        out_ref[:, row, :] = by_high[:modes] + by_high[modes:] + one_pass(high, cover_low, NN)


def call(kernel, shapes, *arrays, flops, spaces=None, room=16):
    whole = pl.BlockSpec(memory_space=pltpu.VMEM)
    size = sum(a.size * a.dtype.itemsize for a in arrays)
    size += sum(a.size * a.dtype.itemsize for a in shapes)
    return pl.pallas_call(
        kernel,
        out_shape=shapes,
        in_specs=spaces or [whole] * len(arrays),
        out_specs=[whole] * len(shapes),
        cost_estimate=pl.CostEstimate(flops=flops, bytes_accessed=size, transcendentals=0),
        compiler_params=pltpu.CompilerParams(vmem_limit_bytes=room * 2**20),
        interpret=INTERPRET,
    )(*arrays)


def local(fields, month_label, row_index, area_table, basis):
    days, lat, lon = fields.shape
    groups = lax.axis_size("days")
    me = lax.axis_index("days")
    wide = -(-(lon + 1) // LANES) * LANES
    modes = basis.shape[0]
    total = days * groups
    n = total // SIDE
    shape = jax.ShapeDtypeStruct

    label = month_label.astype(F32)[None, :, None]
    rows = jnp.pad(jnp.swapaxes(fields, 0, 1).astype(F32), ((0, 0), (0, 0), (0, wide - lon)))
    rows = jnp.where(lax.broadcasted_iota(jnp.int32, rows.shape, 2) == lon, label, rows)
    start = lax.dynamic_index_in_dim(basis, me, axis=1, keepdims=False)
    start = jnp.pad(start, ((0, 0), (0, wide - lon)))
    table_row = lax.dynamic_index_in_dim(row_index, me, keepdims=False)
    where = jnp.stack([me, table_row]).astype(jnp.int32)
    rows, start, where, area_table = lax.optimization_barrier((rows, start, where, area_table))
    rows = lax.all_to_all(rows, "days", 0, 0, tiled=True).reshape(total, wide)

    count = len(lower_blocks(n)) * SIDE + n * modes
    devices = groups * lax.axis_size(SPACE)
    count += -count % devices
    vmem, smem = pl.BlockSpec(memory_space=pltpu.VMEM), pl.BlockSpec(memory_space=pltpu.SMEM)
    tall = total + modes
    pieces, high, low = call(
        functools.partial(products_kernel, lon),
        [shape((count, LANES), F32), shape((tall, wide), BF16), shape((tall, wide), BF16)],
        rows, start, area_table.reshape(1, -1), where,
        flops=2 * 3 * total * tall * wide,
        spaces=[vmem, vmem, vmem, smem],
        room=24,
    )
    pieces = total_everywhere(pieces)
    products, pcs, raw, cover = call(
        cover_kernel,
        [shape((total, total), F32), shape((modes, total), F32), shape((modes, total), F32),
         shape((modes, lon), F32)],
        pieces, high, low,
        flops=2 * 3 * modes * total * (total + wide),
    )

    def shifted(by):
        return lax.ppermute(cover, "days", [(i, (i + by) % groups) for i in range(groups)])

    across, before, after = shifted(2), shifted(1), shifted(3)
    both, last = call(
        chain_kernel,
        [shape((modes, 2 * modes), F32), shape((modes, total), F32)],
        products, pcs, raw,
        flops=2 * 6 * modes * total * (total + 8 * modes),
    )
    eofs, = call(
        patterns_kernel,
        [shape((modes, lat, lon), F32)],
        both, cover, before, after, across, where,
        flops=2 * 3 * modes * modes * lat * lon,
        spaces=[vmem] * 5 + [smem],
    )
    return (eofs, lax.dynamic_slice_in_dim(last, me * days, days, axis=1).T)


def solution(mesh):
    space = mesh.shape["space"]
    cores = 2
    around = 4 if space % 8 == 0 else 1
    parts = Mesh(
        mesh.devices.reshape(mesh.shape["days"], space // around // cores, around, cores),
        ("days", *SPACE),
    )
    placed = (
        P("days", SPACE, None), P("days"), P(SPACE), P(), P(None, SPACE, None),
    )
    return jax.shard_map(
        local,
        mesh=parts,
        in_specs=placed,
        out_specs=(P(None, SPACE, None), P("days", None)),
        check_vma=False,
    )
```

```python
import functools

import jax
import jax.numpy as jnp
from jax import lax
from jax.experimental import pallas as pl
from jax.experimental.pallas import tpu as pltpu
from jax.sharding import Mesh, PartitionSpec as P

LANES = 128
SIDE = 128
HIGH = lax.Precision.HIGHEST
F32 = jnp.float32
BF16 = jnp.bfloat16
INTERPRET = False
SPACE = ("z", "x", "core")
STAGES = ("core", ("days", "x"))
ALONG = "z"


def to_each(shard, axis):
    devices = lax.axis_size(axis)
    return lax.all_to_all(
        jnp.broadcast_to(shard[None], (devices, *shard.shape)), axis, 0, 0, tiled=True
    )


def dot(a, b, dims, precision=HIGH):
    return lax.dot_general(a, b, (dims, ((), ())), precision=precision, preferred_element_type=F32)


def one_pass(a, b, dims):
    return dot(a, b, dims, lax.Precision.DEFAULT)


NT = ((1,), (1,))
NN = ((1,), (0,))


def split(x):
    high = x.astype(BF16)
    return high, (x - high.astype(F32)).astype(BF16)


def lower_blocks(n):
    return [(r, c) for c in range(n) for r in range(c, n)]


def payload_rows(days, lon):
    full, spare = divmod(lon, LANES)
    short = days * spare // LANES
    assert LANES % spare == 0 and short * LANES == days * spare and short % 8 == 0
    return full, spare, short, full * days + short + 8


def side_by_side(left, short):
    parts = left.shape[0] // short
    packed = left[:short]
    for g in range(1, parts):
        packed += pltpu.roll(left[g * short : (g + 1) * short], g * (LANES // parts), 1)
    return packed


def one_below_another(packed, parts):
    lane = lax.broadcasted_iota(jnp.int32, packed.shape, 1)
    width = LANES // parts
    pieces = [pltpu.roll(packed, LANES - g * width, 1) if g else packed for g in range(parts)]
    return jnp.concatenate([jnp.where(lane < width, piece, 0.0) for piece in pieces], axis=0)


def payload_kernel(fields_ref, label_ref, out_ref):
    lat, days, lon = fields_ref.shape
    full, spare, short, count = payload_rows(days, lon)
    label = label_ref[...].astype(F32)
    rest = jnp.zeros((1, LANES - (days - LANES)), F32)
    labels = jnp.concatenate(
        [label[:, :LANES], jnp.concatenate([label[:, LANES:], rest], axis=1), jnp.zeros((6, LANES), F32)]
    )
    for row in range(lat):
        for t in range(full):
            tile = fields_ref[row, :, t * LANES : (t + 1) * LANES].astype(F32)
            out_ref[row, t * days : (t + 1) * days] = tile
        left = fields_ref[row, :, full * LANES :].astype(F32)
        left = jnp.concatenate([left, jnp.zeros((days, LANES - spare), F32)], axis=1)
        out_ref[row, full * days : full * days + short] = side_by_side(left, short)
        out_ref[row, count - 8 :] = labels


def products_kernel(
    days, lon, rows_ref, base_ref, table_ref, row_ref, where_ref,
    out_ref, high_ref, low_ref,
):
    groups = rows_ref.shape[0]
    modes, wide = base_ref.shape
    full, spare, short, count = payload_rows(days, lon)
    total = groups * days
    n = total // SIDE

    def fields_of(d):
        tiles = [rows_ref[d, t * days : (t + 1) * days] for t in range(full)]
        packed = rows_ref[d, full * days : full * days + short]
        return jnp.concatenate(tiles + [one_below_another(packed, days // short)], axis=1)

    def hot_of(d):
        labels = rows_ref[d, count - 8 :]
        label = jnp.concatenate([labels[:1], labels[1:2]], axis=1)
        month = lax.broadcasted_iota(jnp.int32, (LANES, 2 * LANES), 0)
        day = lax.broadcasted_iota(jnp.int32, (LANES, 2 * LANES), 1)
        hit = ((month % 16).astype(F32) == label) & (month < 48) & (day < days)
        return jnp.where(hit, 1.0, 0.0)

    hots = [hot_of(d) for d in range(groups)]
    counts = sum(jnp.sum(hot[:16], axis=1, keepdims=True) for hot in hots)
    sums = sum(
        one_pass(hot[:16, :days].astype(BF16), fields_of(d).astype(BF16), NN)
        for d, hot in enumerate(hots)
    )
    climate = sums / jnp.maximum(counts, 1.0)
    first = climate.astype(BF16)
    rest = climate - first.astype(F32)
    second = rest.astype(BF16)
    third = (rest - second.astype(F32)).astype(BF16)
    terms = jnp.concatenate(
        [first.astype(F32), second.astype(F32), third.astype(F32), jnp.zeros((LANES - 48, wide), F32)]
    ).astype(BF16)
    entry = lax.broadcasted_iota(jnp.int32, table_ref.shape, 1)
    own = jnp.where(entry == row_ref[where_ref[0]], table_ref[...], 0.0)
    scale = jnp.sqrt(jnp.sum(own, axis=1, keepdims=True))
    for d in range(groups):
        part = slice(d * days, (d + 1) * days)
        hot = jnp.transpose(hots[d])[:days].astype(BF16)
        weighted = (fields_of(d) - one_pass(hot, terms, NN)) * scale
        high, low = split(weighted)
        high_ref[part] = high
        low_ref[part] = low
    days = total
    high_ref[days:] = base_ref[...]
    low_ref[days:] = jnp.zeros((modes, wide), BF16)
    order = lower_blocks(n)
    for c in range(0, n, 2):
        group = slice(c * SIDE, min(c + 2, n) * SIDE)
        below = slice(c * SIDE, days + modes)
        product = one_pass(high_ref[below], high_ref[group], NT)
        product += one_pass(high_ref[below], low_ref[group], NT)
        product += one_pass(low_ref[below], high_ref[group], NT)
        for k in range(c, min(c + 2, n)):
            lanes = slice((k - c) * SIDE, (k - c + 1) * SIDE)
            for r in range(k, n):
                at = order.index((r, k)) * SIDE
                out_ref[at : at + SIDE] = product[(r - c) * SIDE : (r - c + 1) * SIDE, lanes]
            at = len(order) * SIDE + k * modes
            out_ref[at : at + modes] = product[days - c * SIDE :, lanes]
    at = len(order) * SIDE + n * modes
    if at < out_ref.shape[0]:
        out_ref[at:] = jnp.zeros((out_ref.shape[0] - at, LANES), F32)


def assemble(rows_ref, products_ref, pcs_ref):
    modes, days = pcs_ref.shape
    n = days // SIDE
    order = lower_blocks(n)
    for at, (r, c) in enumerate(order):
        block = rows_ref[at * SIDE : (at + 1) * SIDE] * (1.0 / days)
        rows, lanes = slice(r * SIDE, (r + 1) * SIDE), slice(c * SIDE, (c + 1) * SIDE)
        products_ref[rows, lanes] = block
        if r > c:
            products_ref[lanes, rows] = block.T
    at = len(order) * SIDE
    for i in range(n):
        pcs_ref[:, i * SIDE : (i + 1) * SIDE] = rows_ref[at : at + modes]
        at += modes


def cover_kernel(lon, rows_ref, high_ref, low_ref, cover_ref, products_ref, pcs_ref):
    modes, days = pcs_ref.shape
    assemble(rows_ref, products_ref, pcs_ref)
    raw = dot(pcs_ref[...], products_ref[...], NN)
    high, low = split(raw * (1.0 / days))
    both = jnp.concatenate([high, low], axis=0)
    by_high = one_pass(both, high_ref[:days], NN)
    by_low = one_pass(high, low_ref[:days], NN)
    cover = by_high[:modes] + by_high[modes:] + by_low
    full, _, short, _ = payload_rows(modes, lon)
    for t in range(full):
        cover_ref[t * modes : (t + 1) * modes] = cover[:, t * LANES : (t + 1) * LANES]
    cover_ref[full * modes :] = side_by_side(cover[:, full * LANES :], short)


def inverse_factor(gram, modes):
    row = lax.broadcasted_iota(jnp.int32, gram.shape, 0)
    lane = lax.broadcasted_iota(jnp.int32, gram.shape, 1)
    whole = jnp.where(lane < modes, jnp.where(row == lane, 1.0, 0.0), gram)
    blocks = [whole[at : at + 8] for at in range(0, modes, 8)]
    sub = lax.broadcasted_iota(jnp.int32, (8, gram.shape[1]), 0)
    for j in range(modes):
        own, at = divmod(j, 8)
        pivot_row = blocks[own][at : at + 1]
        scaled = pivot_row / pivot_row[:, modes + j : modes + j + 1]
        for b in range(own, modes // 8):
            if b == own and at == 7:
                continue
            column = blocks[b][:, modes + j : modes + j + 1]
            step = column * scaled
            if b == own:
                step = jnp.where(sub > at, step, 0.0)
            blocks[b] = blocks[b] - step
    whole = jnp.concatenate(blocks, axis=0)
    pivots = jnp.sum(jnp.where(lane == row + modes, whole, 0.0), axis=1, keepdims=True)
    return jnp.where(lane < modes, whole / jnp.sqrt(pivots), 0.0)


def chain_kernel(rows_ref, both_ref, last_ref, products_ref, pcs_ref):
    modes, days = pcs_ref.shape
    assemble(rows_ref, products_ref, pcs_ref)
    nothing = jnp.zeros((modes, days), F32)
    raw = dot(pcs_ref[...], products_ref[...], NN)
    gram = dot(pcs_ref[...], jnp.concatenate([nothing, raw]), NT) * (1.0 / days)
    first = inverse_factor(gram, modes)
    pcs = dot(first, jnp.concatenate([raw, nothing]), NN)
    raw = dot(pcs, products_ref[...], NN)
    gram = dot(pcs, jnp.concatenate([nothing, raw]), NT) * (1.0 / days)
    second = inverse_factor(gram, modes)
    last_ref[...] = dot(second, jnp.concatenate([raw, nothing]), NN)
    both_ref[...] = dot(second, jnp.concatenate([first, jnp.zeros_like(first)]), NN)


def patterns_kernel(both_ref, own_ref, before_ref, after_ref, across_ref, where_ref, out_ref):
    modes, lat, lon = out_ref.shape
    me = where_ref[0]
    full, _, short, _ = payload_rows(modes, lon)
    high, low = split(both_ref[:, :modes])
    stacked = jnp.concatenate([high, low], axis=0)
    for row in range(lat):
        ahead = lax.rem(row - me + lat, lat)
        cover = jnp.where(
            ahead == 0,
            own_ref[...],
            jnp.where(ahead == 1, after_ref[...], jnp.where(ahead == 2, across_ref[...], before_ref[...])),
        )
        tiles = [cover[t * modes : (t + 1) * modes] for t in range(full)]
        tiles.append(one_below_another(cover[full * modes :], modes // short))
        cover_high, cover_low = split(jnp.concatenate(tiles, axis=1))
        by_high = one_pass(stacked, cover_high, NN)
        rows = by_high[:modes] + by_high[modes:] + one_pass(high, cover_low, NN)
        out_ref[:, row, :] = rows[:, :lon]


def call(kernel, shapes, *arrays, flops, spaces=None, scratch=(), room=16):
    whole = pl.BlockSpec(memory_space=pltpu.VMEM)
    size = sum(a.size * a.dtype.itemsize for a in arrays)
    size += sum(a.size * a.dtype.itemsize for a in shapes)
    return pl.pallas_call(
        kernel,
        out_shape=shapes,
        in_specs=spaces or [whole] * len(arrays),
        out_specs=[whole] * len(shapes),
        scratch_shapes=scratch,
        cost_estimate=pl.CostEstimate(flops=flops, bytes_accessed=size, transcendentals=0),
        compiler_params=pltpu.CompilerParams(vmem_limit_bytes=room * 2**20),
        interpret=INTERPRET,
    )(*arrays)


def sum_kernel(tiles_ref, out_ref):
    out_ref[...] = jnp.broadcast_to(jnp.sum(tiles_ref[...], axis=0), out_ref.shape)


def summed(tiles, copies=0):
    tail = tiles.shape[1:]
    out, = call(
        sum_kernel,
        [jax.ShapeDtypeStruct((copies, *tail) if copies else tail, F32)],
        tiles,
        flops=tiles.size,
        room=8,
    )
    return out


def total_everywhere(rows):
    def exchanged(tiles, axis):
        return lax.all_to_all(tiles, axis, 0, 0, tiled=True)

    near, plane = STAGES
    rows = summed(exchanged(rows.reshape(lax.axis_size(near), -1, LANES), near))
    tiles = exchanged(rows.reshape(lax.axis_size(plane), -1, LANES), plane)
    tiles = exchanged(summed(tiles, lax.axis_size(ALONG)), ALONG)
    rows = exchanged(summed(tiles, lax.axis_size(plane)), plane)
    return to_each(rows.reshape(-1, LANES), near).reshape(-1, LANES)


def local(fields, month_label, row_index, area_table, basis):
    days, lat, lon = fields.shape
    groups = lax.axis_size("days")
    me = lax.axis_index("days")
    wide = -(-(lon + 1) // LANES) * LANES
    modes = basis.shape[0]
    total = days * groups
    n = total // SIDE
    shape = jax.ShapeDtypeStruct

    rows, = call(
        payload_kernel,
        [shape((lat, payload_rows(days, lon)[-1], LANES), F32)],
        jnp.swapaxes(fields, 0, 1), month_label.reshape(1, -1),
        flops=fields.size,
    )
    start = lax.dynamic_index_in_dim(basis, me, axis=1, keepdims=False)
    start = jnp.pad(start, ((0, 0), (0, wide - lon)))
    rows, start = lax.optimization_barrier((rows, start))
    rows = lax.all_to_all(rows, "days", 0, 0, tiled=True)

    where = me.astype(jnp.int32).reshape(1)
    count = len(lower_blocks(n)) * SIDE + n * modes
    devices = groups * lax.axis_size(SPACE)
    count += -count % devices
    vmem, smem = pl.BlockSpec(memory_space=pltpu.VMEM), pl.BlockSpec(memory_space=pltpu.SMEM)
    tall = total + modes
    pieces, high, low = call(
        functools.partial(products_kernel, days, lon),
        [shape((count, LANES), F32), shape((tall, wide), BF16), shape((tall, wide), BF16)],
        rows, start, area_table.reshape(1, -1), row_index, where,
        flops=2 * 3 * total * tall * wide,
        spaces=[vmem, vmem, vmem, smem, smem],
        room=24,
    )
    pieces = total_everywhere(pieces)
    matrices = [pltpu.VMEM((total, total), F32), pltpu.VMEM((modes, total), F32)]
    cover, = call(
        functools.partial(cover_kernel, lon),
        [shape((modes * lon // LANES, LANES), F32)],
        pieces, high, low,
        flops=2 * 3 * modes * total * (total + wide),
        scratch=matrices,
    )

    def shifted(by):
        return lax.ppermute(cover, "days", [(i, (i + by) % groups) for i in range(groups)])

    across, before, after = shifted(2), shifted(1), shifted(3)
    both, last = call(
        chain_kernel,
        [shape((modes, 2 * modes), F32), shape((modes, total), F32)],
        pieces,
        flops=2 * 6 * modes * total * (total + 8 * modes),
        scratch=matrices,
    )
    eofs, = call(
        patterns_kernel,
        [shape((modes, lat, lon), F32)],
        both, cover, before, after, across, where,
        flops=2 * 3 * modes * modes * lat * lon,
        spaces=[vmem] * 5 + [smem],
    )
    return (eofs, lax.dynamic_slice_in_dim(last, me * days, days, axis=1).T)


def solution(mesh):
    space = mesh.shape["space"]
    cores = 2
    around = 4 if space % 8 == 0 else 1
    parts = Mesh(
        mesh.devices.reshape(mesh.shape["days"], space // around // cores, around, cores),
        ("days", *SPACE),
    )
    placed = (
        P("days", SPACE, None), P("days"), P(SPACE), P(), P(None, SPACE, None),
    )
    return jax.shard_map(
        local,
        mesh=parts,
        in_specs=placed,
        out_specs=(P(None, SPACE, None), P("days", None)),
        check_vma=False,
    )
```

```python
import functools

import jax
import jax.numpy as jnp
from jax import lax
from jax.experimental import pallas as pl
from jax.experimental.pallas import tpu as pltpu
from jax.sharding import Mesh, PartitionSpec as P

LANES = 128
SIDE = 128
HIGH = lax.Precision.HIGHEST
F32 = jnp.float32
BF16 = jnp.bfloat16
INTERPRET = False
SPACE = ("z", "x", "core")
STAGES = ("core", ("days", "x"))
ALONG = "z"


def to_each(shard, axis):
    devices = lax.axis_size(axis)
    return lax.all_to_all(
        jnp.broadcast_to(shard[None], (devices, *shard.shape)), axis, 0, 0, tiled=True
    )


def dot(a, b, dims, precision=HIGH):
    return lax.dot_general(a, b, (dims, ((), ())), precision=precision, preferred_element_type=F32)


def one_pass(a, b, dims):
    return dot(a, b, dims, lax.Precision.DEFAULT)


NT = ((1,), (1,))
NN = ((1,), (0,))


def split(x):
    high = x.astype(BF16)
    return high, (x - high.astype(F32)).astype(BF16)


HALF = SIDE // 2


def lower_blocks(n):
    below, at = {}, 0
    for c in range(n):
        for r in range(c, n):
            below[r, c] = at
            at += SIDE if r > c else HALF
    return below, at


def positions(shape):
    return (lax.broadcasted_iota(jnp.int32, shape, 0), lax.broadcasted_iota(jnp.int32, shape, 1))


def folded(block):
    top, bottom = block[:HALF], block[HALF:]
    row, lane = positions(top.shape)
    rows = jnp.where(row > lane - HALF, jnp.where(lane < HALF, bottom, pltpu.roll(top, HALF, 1)), bottom)
    diagonal = jnp.sum(jnp.where(row == lane, top, 0.0), axis=0, keepdims=True)
    return rows, diagonal


def unfolded(rows, diagonal):
    row, lane = positions(rows.shape)
    top = jnp.where(lane < row, pltpu.roll(rows, HALF, 1), jnp.where(lane == row, diagonal, 0.0))
    bottom = jnp.where((lane < HALF) | (row <= lane - HALF), rows, 0.0)
    lower = jnp.concatenate([top, bottom], axis=0)
    row, lane = positions(lower.shape)
    return lower + jnp.where(row == lane, 0.0, lower).T


def sum_rows(n, modes):
    return lower_blocks(n)[1] + n * modes + 8


def payload_rows(days, lon):
    full, spare = divmod(lon, LANES)
    short = days * spare // LANES
    assert LANES % spare == 0 and short * LANES == days * spare and short % 8 == 0
    return full, spare, short, full * days + short + 8


def side_by_side(left, short):
    parts = left.shape[0] // short
    packed = left[:short]
    for g in range(1, parts):
        packed += pltpu.roll(left[g * short : (g + 1) * short], g * (LANES // parts), 1)
    return packed


def one_below_another(packed, parts):
    lane = lax.broadcasted_iota(jnp.int32, packed.shape, 1)
    width = LANES // parts
    pieces = [pltpu.roll(packed, LANES - g * width, 1) if g else packed for g in range(parts)]
    return jnp.concatenate([jnp.where(lane < width, piece, 0.0) for piece in pieces], axis=0)


def payload_kernel(fields_ref, label_ref, out_ref):
    lat, days, lon = fields_ref.shape
    full, spare, short, count = payload_rows(days, lon)
    label = label_ref[...].astype(F32)
    rest = jnp.zeros((1, LANES - (days - LANES)), F32)
    labels = jnp.concatenate(
        [label[:, :LANES], jnp.concatenate([label[:, LANES:], rest], axis=1), jnp.zeros((6, LANES), F32)]
    )
    for row in range(lat):
        for t in range(full):
            tile = fields_ref[row, :, t * LANES : (t + 1) * LANES].astype(F32)
            out_ref[row, t * days : (t + 1) * days] = tile
        left = fields_ref[row, :, full * LANES :].astype(F32)
        left = jnp.concatenate([left, jnp.zeros((days, LANES - spare), F32)], axis=1)
        out_ref[row, full * days : full * days + short] = side_by_side(left, short)
        out_ref[row, count - 8 :] = labels


def products_kernel(
    days, lon, rows_ref, base_ref, table_ref, row_ref, where_ref,
    out_ref, high_ref, low_ref,
):
    groups = rows_ref.shape[0]
    modes, wide = base_ref.shape
    full, spare, short, count = payload_rows(days, lon)
    total = groups * days
    n = total // SIDE

    def fields_of(d):
        tiles = [rows_ref[d, t * days : (t + 1) * days] for t in range(full)]
        packed = rows_ref[d, full * days : full * days + short]
        return jnp.concatenate(tiles + [one_below_another(packed, days // short)], axis=1)

    def hot_of(d):
        labels = rows_ref[d, count - 8 :]
        label = jnp.concatenate([labels[:1], labels[1:2]], axis=1)
        month = lax.broadcasted_iota(jnp.int32, (LANES, 2 * LANES), 0)
        day = lax.broadcasted_iota(jnp.int32, (LANES, 2 * LANES), 1)
        hit = ((month % 16).astype(F32) == label) & (month < 48) & (day < days)
        return jnp.where(hit, 1.0, 0.0)

    hots = [hot_of(d) for d in range(groups)]
    counts = sum(jnp.sum(hot[:16], axis=1, keepdims=True) for hot in hots)
    sums = sum(
        one_pass(hot[:16, :days].astype(BF16), fields_of(d).astype(BF16), NN)
        for d, hot in enumerate(hots)
    )
    climate = sums / jnp.maximum(counts, 1.0)
    first = climate.astype(BF16)
    rest = climate - first.astype(F32)
    second = rest.astype(BF16)
    third = (rest - second.astype(F32)).astype(BF16)
    terms = jnp.concatenate(
        [first.astype(F32), second.astype(F32), third.astype(F32), jnp.zeros((LANES - 48, wide), F32)]
    ).astype(BF16)
    entry = lax.broadcasted_iota(jnp.int32, table_ref.shape, 1)
    own = jnp.where(entry == row_ref[where_ref[0]], table_ref[...], 0.0)
    scale = jnp.sqrt(jnp.sum(own, axis=1, keepdims=True))
    for d in range(groups):
        part = slice(d * days, (d + 1) * days)
        hot = jnp.transpose(hots[d])[:days].astype(BF16)
        weighted = (fields_of(d) - one_pass(hot, terms, NN)) * scale
        high, low = split(weighted)
        high_ref[part] = high
        low_ref[part] = low
    days = total
    high_ref[days:] = base_ref[...]
    low_ref[days:] = jnp.zeros((modes, wide), BF16)
    below, end = lower_blocks(n)
    diagonals = []
    for c in range(0, n, 2):
        group = slice(c * SIDE, min(c + 2, n) * SIDE)
        under = slice(c * SIDE, days + modes)
        product = one_pass(high_ref[under], high_ref[group], NT)
        product += one_pass(high_ref[under], low_ref[group], NT)
        product += one_pass(low_ref[under], high_ref[group], NT)
        for k in range(c, min(c + 2, n)):
            lanes = slice((k - c) * SIDE, (k - c + 1) * SIDE)
            for r in range(k, n):
                at = below[r, k]
                block = product[(r - c) * SIDE : (r - c + 1) * SIDE, lanes]
                if r > k:
                    out_ref[at : at + SIDE] = block
                else:
                    out_ref[at : at + HALF], diagonal = folded(block)
                    diagonals.append(diagonal)
            at = end + k * modes
            out_ref[at : at + modes] = product[days - c * SIDE :, lanes]
    at = end + n * modes
    out_ref[at : at + 8] = jnp.concatenate(diagonals + [jnp.zeros((8 - n, LANES), F32)], axis=0)
    at += 8
    if at < out_ref.shape[0]:
        out_ref[at:] = jnp.zeros((out_ref.shape[0] - at, LANES), F32)


def assemble(rows_ref, products_ref, pcs_ref):
    modes, days = pcs_ref.shape
    n = days // SIDE
    below, end = lower_blocks(n)
    diagonals = rows_ref[end + n * modes : end + n * modes + 8]
    for (r, c), at in below.items():
        rows, lanes = slice(r * SIDE, (r + 1) * SIDE), slice(c * SIDE, (c + 1) * SIDE)
        if r > c:
            block = rows_ref[at : at + SIDE] * (1.0 / days)
            products_ref[rows, lanes] = block
            products_ref[lanes, rows] = block.T
        else:
            block = unfolded(rows_ref[at : at + HALF], diagonals[r : r + 1])
            products_ref[rows, lanes] = block * (1.0 / days)
    for i in range(n):
        at = end + i * modes
        pcs_ref[:, i * SIDE : (i + 1) * SIDE] = rows_ref[at : at + modes]


def cover_kernel(lon, rows_ref, high_ref, low_ref, cover_ref, products_ref, pcs_ref):
    modes, days = pcs_ref.shape
    assemble(rows_ref, products_ref, pcs_ref)
    raw = dot(pcs_ref[...], products_ref[...], NN)
    high, low = split(raw * (1.0 / days))
    both = jnp.concatenate([high, low], axis=0)
    by_high = one_pass(both, high_ref[:days], NN)
    by_low = one_pass(high, low_ref[:days], NN)
    cover = by_high[:modes] + by_high[modes:] + by_low
    full, _, short, _ = payload_rows(modes, lon)
    for t in range(full):
        cover_ref[t * modes : (t + 1) * modes] = cover[:, t * LANES : (t + 1) * LANES]
    cover_ref[full * modes :] = side_by_side(cover[:, full * LANES :], short)


def inverse_factor(gram, modes):
    row = lax.broadcasted_iota(jnp.int32, gram.shape, 0)
    lane = lax.broadcasted_iota(jnp.int32, gram.shape, 1)
    whole = jnp.where(lane < modes, jnp.where(row == lane, 1.0, 0.0), gram)
    blocks = [whole[at : at + 8] for at in range(0, modes, 8)]
    sub = lax.broadcasted_iota(jnp.int32, (8, gram.shape[1]), 0)
    for j in range(modes):
        own, at = divmod(j, 8)
        pivot_row = blocks[own][at : at + 1]
        scaled = pivot_row / pivot_row[:, modes + j : modes + j + 1]
        for b in range(own, modes // 8):
            if b == own and at == 7:
                continue
            column = blocks[b][:, modes + j : modes + j + 1]
            step = column * scaled
            if b == own:
                step = jnp.where(sub > at, step, 0.0)
            blocks[b] = blocks[b] - step
    whole = jnp.concatenate(blocks, axis=0)
    pivots = jnp.sum(jnp.where(lane == row + modes, whole, 0.0), axis=1, keepdims=True)
    return jnp.where(lane < modes, whole / jnp.sqrt(pivots), 0.0)


def chain_kernel(rows_ref, both_ref, last_ref, products_ref, pcs_ref):
    modes, days = pcs_ref.shape
    assemble(rows_ref, products_ref, pcs_ref)
    nothing = jnp.zeros((modes, days), F32)
    raw = dot(pcs_ref[...], products_ref[...], NN)
    gram = dot(pcs_ref[...], jnp.concatenate([nothing, raw]), NT) * (1.0 / days)
    first = inverse_factor(gram, modes)
    pcs = dot(first, jnp.concatenate([raw, nothing]), NN)
    raw = dot(pcs, products_ref[...], NN)
    gram = dot(pcs, jnp.concatenate([nothing, raw]), NT) * (1.0 / days)
    second = inverse_factor(gram, modes)
    last_ref[...] = dot(second, jnp.concatenate([raw, nothing]), NN)
    both_ref[...] = dot(second, jnp.concatenate([first, jnp.zeros_like(first)]), NN)


def patterns_kernel(both_ref, own_ref, before_ref, after_ref, across_ref, where_ref, out_ref):
    modes, lat, lon = out_ref.shape
    me = where_ref[0]
    full, _, short, _ = payload_rows(modes, lon)
    high, low = split(both_ref[:, :modes])
    stacked = jnp.concatenate([high, low], axis=0)
    for row in range(lat):
        ahead = lax.rem(row - me + lat, lat)
        cover = jnp.where(
            ahead == 0,
            own_ref[...],
            jnp.where(ahead == 1, after_ref[...], jnp.where(ahead == 2, across_ref[...], before_ref[...])),
        )
        tiles = [cover[t * modes : (t + 1) * modes] for t in range(full)]
        tiles.append(one_below_another(cover[full * modes :], modes // short))
        cover_high, cover_low = split(jnp.concatenate(tiles, axis=1))
        by_high = one_pass(stacked, cover_high, NN)
        rows = by_high[:modes] + by_high[modes:] + one_pass(high, cover_low, NN)
        out_ref[:, row, :] = rows[:, :lon]


def call(kernel, shapes, *arrays, flops, spaces=None, scratch=(), room=16):
    whole = pl.BlockSpec(memory_space=pltpu.VMEM)
    size = sum(a.size * a.dtype.itemsize for a in arrays)
    size += sum(a.size * a.dtype.itemsize for a in shapes)
    return pl.pallas_call(
        kernel,
        out_shape=shapes,
        in_specs=spaces or [whole] * len(arrays),
        out_specs=[whole] * len(shapes),
        scratch_shapes=scratch,
        cost_estimate=pl.CostEstimate(flops=flops, bytes_accessed=size, transcendentals=0),
        compiler_params=pltpu.CompilerParams(vmem_limit_bytes=room * 2**20),
        interpret=INTERPRET,
    )(*arrays)


def sum_kernel(tiles_ref, out_ref):
    out_ref[...] = jnp.broadcast_to(jnp.sum(tiles_ref[...], axis=0), out_ref.shape)


def summed(tiles, copies=0):
    tail = tiles.shape[1:]
    out, = call(
        sum_kernel,
        [jax.ShapeDtypeStruct((copies, *tail) if copies else tail, F32)],
        tiles,
        flops=tiles.size,
        room=8,
    )
    return out


def total_everywhere(rows):
    def exchanged(tiles, axis):
        return lax.all_to_all(tiles, axis, 0, 0, tiled=True)

    near, plane = STAGES
    rows = summed(exchanged(rows.reshape(lax.axis_size(near), -1, LANES), near))
    tiles = exchanged(rows.reshape(lax.axis_size(plane), -1, LANES), plane)
    tiles = exchanged(summed(tiles, lax.axis_size(ALONG)), ALONG)
    rows = exchanged(summed(tiles, lax.axis_size(plane)), plane)
    return to_each(rows.reshape(-1, LANES), near).reshape(-1, LANES)


def local(fields, month_label, row_index, area_table, basis):
    days, lat, lon = fields.shape
    groups = lax.axis_size("days")
    me = lax.axis_index("days")
    wide = -(-(lon + 1) // LANES) * LANES
    modes = basis.shape[0]
    total = days * groups
    n = total // SIDE
    shape = jax.ShapeDtypeStruct

    rows, = call(
        payload_kernel,
        [shape((lat, payload_rows(days, lon)[-1], LANES), F32)],
        jnp.swapaxes(fields, 0, 1), month_label.reshape(1, -1),
        flops=fields.size,
    )
    start = lax.dynamic_index_in_dim(basis, me, axis=1, keepdims=False)
    start = jnp.pad(start, ((0, 0), (0, wide - lon)))
    rows, start = lax.optimization_barrier((rows, start))
    rows = lax.all_to_all(rows, "days", 0, 0, tiled=True)

    where = me.astype(jnp.int32).reshape(1)
    count = sum_rows(n, modes)
    devices = groups * lax.axis_size(SPACE)
    count += -count % devices
    vmem, smem = pl.BlockSpec(memory_space=pltpu.VMEM), pl.BlockSpec(memory_space=pltpu.SMEM)
    tall = total + modes
    pieces, high, low = call(
        functools.partial(products_kernel, days, lon),
        [shape((count, LANES), F32), shape((tall, wide), BF16), shape((tall, wide), BF16)],
        rows, start, area_table.reshape(1, -1), row_index, where,
        flops=2 * 3 * total * tall * wide,
        spaces=[vmem, vmem, vmem, smem, smem],
        room=24,
    )
    pieces = total_everywhere(pieces)
    matrices = [pltpu.VMEM((total, total), F32), pltpu.VMEM((modes, total), F32)]
    cover, = call(
        functools.partial(cover_kernel, lon),
        [shape((modes * lon // LANES, LANES), F32)],
        pieces, high, low,
        flops=2 * 3 * modes * total * (total + wide),
        scratch=matrices,
    )

    def shifted(by):
        return lax.ppermute(cover, "days", [(i, (i + by) % groups) for i in range(groups)])

    across, before, after = shifted(2), shifted(1), shifted(3)
    both, last = call(
        chain_kernel,
        [shape((modes, 2 * modes), F32), shape((modes, total), F32)],
        pieces,
        flops=2 * 6 * modes * total * (total + 8 * modes),
        scratch=matrices,
    )
    eofs, = call(
        patterns_kernel,
        [shape((modes, lat, lon), F32)],
        both, cover, before, after, across, where,
        flops=2 * 3 * modes * modes * lat * lon,
        spaces=[vmem] * 5 + [smem],
    )
    return (eofs, lax.dynamic_slice_in_dim(last, me * days, days, axis=1).T)


def solution(mesh):
    space = mesh.shape["space"]
    cores = 2
    around = 4 if space % 8 == 0 else 1
    parts = Mesh(
        mesh.devices.reshape(mesh.shape["days"], space // around // cores, around, cores),
        ("days", *SPACE),
    )
    placed = (
        P("days", SPACE, None), P("days"), P(SPACE), P(), P(None, SPACE, None),
    )
    return jax.shard_map(
        local,
        mesh=parts,
        in_specs=placed,
        out_specs=(P(None, SPACE, None), P("days", None)),
        check_vma=False,
    )
```

```python
import functools

import jax
import jax.numpy as jnp
from jax import lax
from jax.experimental import pallas as pl
from jax.experimental.pallas import tpu as pltpu
from jax.sharding import Mesh, PartitionSpec as P

LANES = 128
SIDE = 128
HIGH = lax.Precision.HIGHEST
F32 = jnp.float32
BF16 = jnp.bfloat16
INTERPRET = False
SPACE = ("z", "x", "core")
STAGES = ("core", ("days", "x"))
ALONG = "z"


def to_each(shard, axis):
    devices = lax.axis_size(axis)
    return lax.all_to_all(
        jnp.broadcast_to(shard[None], (devices, *shard.shape)), axis, 0, 0, tiled=True
    )


def dot(a, b, dims, precision=HIGH):
    return lax.dot_general(a, b, (dims, ((), ())), precision=precision, preferred_element_type=F32)


def one_pass(a, b, dims):
    return dot(a, b, dims, lax.Precision.DEFAULT)


NT = ((1,), (1,))
NN = ((1,), (0,))


def split(x):
    high = x.astype(BF16)
    return high, (x - high.astype(F32)).astype(BF16)


HALF = SIDE // 2
PANEL = 4


def lower_blocks(n):
    below, at = {}, 0
    for c in range(n):
        for r in range(c, n):
            below[r, c] = at
            at += SIDE if r > c else HALF
    return below, at


def positions(shape):
    return (lax.broadcasted_iota(jnp.int32, shape, 0), lax.broadcasted_iota(jnp.int32, shape, 1))


def folded(block):
    top, bottom = block[:HALF], block[HALF:]
    row, lane = positions(top.shape)
    rows = jnp.where(row > lane - HALF, jnp.where(lane < HALF, bottom, pltpu.roll(top, HALF, 1)), bottom)
    diagonal = jnp.sum(jnp.where(row == lane, top, 0.0), axis=0, keepdims=True)
    return rows, diagonal


def unfolded(rows, diagonal):
    row, lane = positions(rows.shape)
    top = jnp.where(lane < row, pltpu.roll(rows, HALF, 1), jnp.where(lane == row, diagonal, 0.0))
    bottom = jnp.where((lane < HALF) | (row <= lane - HALF), rows, 0.0)
    lower = jnp.concatenate([top, bottom], axis=0)
    row, lane = positions(lower.shape)
    return lower + jnp.where(row == lane, 0.0, lower).T


def sum_rows(n, modes):
    return lower_blocks(n)[1] + n * modes + 8


def payload_rows(days, lon):
    full, spare = divmod(lon, LANES)
    short = days * spare // LANES
    assert LANES % spare == 0 and short * LANES == days * spare and short % 8 == 0
    return full, spare, short, full * days + short + 8


def side_by_side(left, short):
    parts = left.shape[0] // short
    packed = left[:short]
    for g in range(1, parts):
        packed += pltpu.roll(left[g * short : (g + 1) * short], g * (LANES // parts), 1)
    return packed


def one_below_another(packed, parts):
    lane = lax.broadcasted_iota(jnp.int32, packed.shape, 1)
    width = LANES // parts
    pieces = [pltpu.roll(packed, LANES - g * width, 1) if g else packed for g in range(parts)]
    return jnp.concatenate([jnp.where(lane < width, piece, 0.0) for piece in pieces], axis=0)


def payload_kernel(fields_ref, label_ref, out_ref):
    lat, days, lon = fields_ref.shape
    full, spare, short, count = payload_rows(days, lon)
    label = label_ref[...].astype(F32)
    rest = jnp.zeros((1, LANES - (days - LANES)), F32)
    labels = jnp.concatenate(
        [label[:, :LANES], jnp.concatenate([label[:, LANES:], rest], axis=1), jnp.zeros((6, LANES), F32)]
    )
    for row in range(lat):
        for t in range(full):
            tile = fields_ref[row, :, t * LANES : (t + 1) * LANES].astype(F32)
            out_ref[row, t * days : (t + 1) * days] = tile
        left = fields_ref[row, :, full * LANES :].astype(F32)
        left = jnp.concatenate([left, jnp.zeros((days, LANES - spare), F32)], axis=1)
        out_ref[row, full * days : full * days + short] = side_by_side(left, short)
        out_ref[row, count - 8 :] = labels


def products_kernel(
    days, lon, rows_ref, base_ref, table_ref, row_ref, where_ref,
    out_ref, high_ref, low_ref,
):
    groups = rows_ref.shape[0]
    modes, wide = base_ref.shape
    full, spare, short, count = payload_rows(days, lon)
    total = groups * days
    n = total // SIDE

    def fields_of(d):
        tiles = [rows_ref[d, t * days : (t + 1) * days] for t in range(full)]
        packed = rows_ref[d, full * days : full * days + short]
        return jnp.concatenate(tiles + [one_below_another(packed, days // short)], axis=1)

    def hot_of(d):
        labels = rows_ref[d, count - 8 :]
        label = jnp.concatenate([labels[:1], labels[1:2]], axis=1)
        month = lax.broadcasted_iota(jnp.int32, (LANES, 2 * LANES), 0)
        day = lax.broadcasted_iota(jnp.int32, (LANES, 2 * LANES), 1)
        hit = ((month % 16).astype(F32) == label) & (month < 48) & (day < days)
        return jnp.where(hit, 1.0, 0.0)

    hots = [hot_of(d) for d in range(groups)]
    counts = sum(jnp.sum(hot[:16], axis=1, keepdims=True) for hot in hots)
    sums = sum(
        one_pass(hot[:16, :days].astype(BF16), fields_of(d).astype(BF16), NN)
        for d, hot in enumerate(hots)
    )
    climate = sums / jnp.maximum(counts, 1.0)
    first = climate.astype(BF16)
    rest = climate - first.astype(F32)
    second = rest.astype(BF16)
    third = (rest - second.astype(F32)).astype(BF16)
    terms = jnp.concatenate(
        [first.astype(F32), second.astype(F32), third.astype(F32), jnp.zeros((LANES - 48, wide), F32)]
    ).astype(BF16)
    entry = lax.broadcasted_iota(jnp.int32, table_ref.shape, 1)
    own = jnp.where(entry == row_ref[where_ref[0]], table_ref[...], 0.0)
    scale = jnp.sqrt(jnp.sum(own, axis=1, keepdims=True))
    for d in range(groups):
        part = slice(d * days, (d + 1) * days)
        hot = jnp.transpose(hots[d])[:days].astype(BF16)
        weighted = (fields_of(d) - one_pass(hot, terms, NN)) * scale
        high, low = split(weighted)
        high_ref[part] = high
        low_ref[part] = low
    days = total
    high_ref[days:] = base_ref[...]
    low_ref[days:] = jnp.zeros((modes, wide), BF16)
    below, end = lower_blocks(n)
    diagonals = []
    for c in range(0, n, 2):
        group = slice(c * SIDE, min(c + 2, n) * SIDE)
        under = slice(c * SIDE, days + modes)
        product = one_pass(high_ref[under], high_ref[group], NT)
        product += one_pass(high_ref[under], low_ref[group], NT)
        product += one_pass(low_ref[under], high_ref[group], NT)
        for k in range(c, min(c + 2, n)):
            lanes = slice((k - c) * SIDE, (k - c + 1) * SIDE)
            for r in range(k, n):
                at = below[r, k]
                block = product[(r - c) * SIDE : (r - c + 1) * SIDE, lanes]
                if r > k:
                    out_ref[at : at + SIDE] = block
                else:
                    out_ref[at : at + HALF], diagonal = folded(block)
                    diagonals.append(diagonal)
            at = end + k * modes
            out_ref[at : at + modes] = product[days - c * SIDE :, lanes]
    at = end + n * modes
    out_ref[at : at + 8] = jnp.concatenate(diagonals + [jnp.zeros((8 - n, LANES), F32)], axis=0)
    at += 8
    if at < out_ref.shape[0]:
        out_ref[at:] = jnp.zeros((out_ref.shape[0] - at, LANES), F32)


def assemble(rows_ref, products_ref, pcs_ref):
    modes, days = pcs_ref.shape
    n = days // SIDE
    below, end = lower_blocks(n)
    diagonals = rows_ref[end + n * modes : end + n * modes + 8]
    for (r, c), at in below.items():
        rows, lanes = slice(r * SIDE, (r + 1) * SIDE), slice(c * SIDE, (c + 1) * SIDE)
        if r > c:
            block = rows_ref[at : at + SIDE] * (1.0 / days)
            products_ref[rows, lanes] = block
            products_ref[lanes, rows] = block.T
        else:
            block = unfolded(rows_ref[at : at + HALF], diagonals[r : r + 1])
            products_ref[rows, lanes] = block * (1.0 / days)
    for i in range(n):
        at = end + i * modes
        pcs_ref[:, i * SIDE : (i + 1) * SIDE] = rows_ref[at : at + modes]


def cover_kernel(lon, rows_ref, high_ref, low_ref, cover_ref, products_ref, pcs_ref):
    modes, days = pcs_ref.shape
    assemble(rows_ref, products_ref, pcs_ref)
    raw = dot(pcs_ref[...], products_ref[...], NN)
    high, low = split(raw * (1.0 / days))
    both = jnp.concatenate([high, low], axis=0)
    by_high = one_pass(both, high_ref[:days], NN)
    by_low = one_pass(high, low_ref[:days], NN)
    cover = by_high[:modes] + by_high[modes:] + by_low
    full, _, short, _ = payload_rows(modes, lon)
    for t in range(full):
        cover_ref[t * modes : (t + 1) * modes] = cover[:, t * LANES : (t + 1) * LANES]
    cover_ref[full * modes :] = side_by_side(cover[:, full * LANES :], short)


def inverse_factor(gram, modes):
    row = lax.broadcasted_iota(jnp.int32, gram.shape, 0)
    lane = lax.broadcasted_iota(jnp.int32, gram.shape, 1)
    whole = jnp.where(lane < modes, jnp.where(row == lane, 1.0, 0.0), gram)
    blocks = [whole[at : at + 8] for at in range(0, modes, 8)]
    full = (8, gram.shape[1])
    sub = lax.broadcasted_iota(jnp.int32, full, 0)
    for start in range(0, modes, PANEL):
        own, at = divmod(start, 8)
        spots = range(modes + start, modes + start + PANEL)
        rows = [jnp.broadcast_to(blocks[own][at + i : at + i + 1], full) for i in range(PANEL)]
        entry = [
            [jnp.broadcast_to(blocks[own][at + i : at + i + 1, spot : spot + 1], full) for spot in spots]
            for i in range(PANEL)
        ]
        factor = [[None] * PANEL for _ in range(PANEL)]
        scaled = []
        for k in range(PANEL):
            inverse = 1.0 / entry[k][k]
            for i in range(k + 1, PANEL):
                factor[i][k] = entry[i][k] * inverse
            for i in range(k + 1, PANEL):
                for m in range(k + 1, i + 1):
                    entry[i][m] = entry[i][m] - factor[i][k] * entry[m][k]
                rows[i] = rows[i] - factor[i][k] * rows[k]
            scaled.append(rows[k] * inverse)
        for b in range(own, modes // 8):
            columns = []
            step = None
            for k, spot in enumerate(spots):
                column = jnp.broadcast_to(blocks[b][:, spot : spot + 1], full)
                for m in range(k):
                    column = column - columns[m] * factor[k][m]
                columns.append(column)
                if b == own:
                    column = jnp.where(sub > at + k, column, 0.0)
                step = column * scaled[k] if step is None else step + column * scaled[k]
            blocks[b] = blocks[b] - step
    whole = jnp.concatenate(blocks, axis=0)
    pivots = jnp.sum(jnp.where(lane == row + modes, whole, 0.0), axis=1, keepdims=True)
    return jnp.where(lane < modes, whole / jnp.sqrt(pivots), 0.0)


def first_kernel(rows_ref, first_ref, new_pcs_ref, raw_ref, products_ref, pcs_ref):
    modes, days = pcs_ref.shape
    assemble(rows_ref, products_ref, pcs_ref)
    nothing = jnp.zeros((modes, days), F32)
    raw = dot(pcs_ref[...], products_ref[...], NN)
    gram = dot(pcs_ref[...], jnp.concatenate([nothing, raw]), NT) * (1.0 / days)
    first = inverse_factor(gram, modes)
    pcs = dot(first, jnp.concatenate([raw, nothing]), NN)
    first_ref[...] = first
    new_pcs_ref[...] = pcs
    raw_ref[...] = dot(pcs, products_ref[...], NN)


def second_kernel(first_ref, pcs_ref, raw_ref, both_ref, last_ref):
    modes, days = pcs_ref.shape
    nothing = jnp.zeros((modes, days), F32)
    raw = raw_ref[...]
    gram = dot(pcs_ref[...], jnp.concatenate([nothing, raw]), NT) * (1.0 / days)
    second = inverse_factor(gram, modes)
    first = first_ref[...]
    last_ref[...] = dot(second, jnp.concatenate([raw, nothing]), NN)
    both_ref[...] = dot(second, jnp.concatenate([first, jnp.zeros_like(first)]), NN)


def patterns_kernel(both_ref, own_ref, before_ref, after_ref, upper_ref, lower_ref, where_ref, out_ref):
    modes, lat, lon = out_ref.shape
    me = where_ref[0]
    full, _, short, _ = payload_rows(modes, lon)
    high, low = split(both_ref[:, :modes])
    stacked = jnp.concatenate([high, low], axis=0)
    across = jnp.concatenate([upper_ref[...], lower_ref[...]], axis=0)
    for row in range(lat):
        ahead = lax.rem(row - me + lat, lat)
        cover = jnp.where(
            ahead == 0,
            own_ref[...],
            jnp.where(ahead == 1, after_ref[...], jnp.where(ahead == 2, across, before_ref[...])),
        )
        tiles = [cover[t * modes : (t + 1) * modes] for t in range(full)]
        tiles.append(one_below_another(cover[full * modes :], modes // short))
        cover_high, cover_low = split(jnp.concatenate(tiles, axis=1))
        by_high = one_pass(stacked, cover_high, NN)
        rows = by_high[:modes] + by_high[modes:] + one_pass(high, cover_low, NN)
        out_ref[:, row, :] = rows[:, :lon]


def call(kernel, shapes, *arrays, flops, spaces=None, scratch=(), room=16):
    whole = pl.BlockSpec(memory_space=pltpu.VMEM)
    size = sum(a.size * a.dtype.itemsize for a in arrays)
    size += sum(a.size * a.dtype.itemsize for a in shapes)
    return pl.pallas_call(
        kernel,
        out_shape=shapes,
        in_specs=spaces or [whole] * len(arrays),
        out_specs=[whole] * len(shapes),
        scratch_shapes=scratch,
        cost_estimate=pl.CostEstimate(flops=flops, bytes_accessed=size, transcendentals=0),
        compiler_params=pltpu.CompilerParams(vmem_limit_bytes=room * 2**20),
        interpret=INTERPRET,
    )(*arrays)


def sum_kernel(tiles_ref, out_ref):
    out_ref[...] = jnp.broadcast_to(jnp.sum(tiles_ref[...], axis=0), out_ref.shape)


def summed(tiles, copies=0):
    tail = tiles.shape[1:]
    out, = call(
        sum_kernel,
        [jax.ShapeDtypeStruct((copies, *tail) if copies else tail, F32)],
        tiles,
        flops=tiles.size,
        room=8,
    )
    return out


def total_everywhere(rows):
    def exchanged(tiles, axis):
        return lax.all_to_all(tiles, axis, 0, 0, tiled=True)

    near, plane = STAGES
    rows = summed(exchanged(rows.reshape(lax.axis_size(near), -1, LANES), near))
    tiles = exchanged(rows.reshape(lax.axis_size(plane), -1, LANES), plane)
    tiles = exchanged(summed(tiles, lax.axis_size(ALONG)), ALONG)
    rows = exchanged(summed(tiles, lax.axis_size(plane)), plane)
    return to_each(rows.reshape(-1, LANES), near).reshape(-1, LANES)


def local(fields, month_label, row_index, area_table, basis):
    days, lat, lon = fields.shape
    groups = lax.axis_size("days")
    me = lax.axis_index("days")
    wide = -(-(lon + 1) // LANES) * LANES
    modes = basis.shape[0]
    total = days * groups
    n = total // SIDE
    shape = jax.ShapeDtypeStruct

    fields = jnp.swapaxes(fields, 0, 1)
    rows, = call(
        payload_kernel,
        [shape((lat, payload_rows(days, lon)[-1], LANES), F32)],
        fields, month_label.reshape(1, -1),
        flops=fields.size,
    )
    start = lax.dynamic_index_in_dim(basis, me, axis=1, keepdims=False)
    start = jnp.pad(start, ((0, 0), (0, wide - lon)))
    rows, start = lax.optimization_barrier((rows, start))
    rows = lax.all_to_all(rows, "days", 0, 0, tiled=True)

    where = me.astype(jnp.int32).reshape(1)
    count = sum_rows(n, modes)
    devices = groups * lax.axis_size(SPACE)
    count += -count % devices
    vmem, smem = pl.BlockSpec(memory_space=pltpu.VMEM), pl.BlockSpec(memory_space=pltpu.SMEM)
    tall = total + modes
    pieces, high, low = call(
        functools.partial(products_kernel, days, lon),
        [shape((count, LANES), F32), shape((tall, wide), BF16), shape((tall, wide), BF16)],
        rows, start, area_table.reshape(1, -1), row_index, where,
        flops=2 * 3 * total * tall * wide,
        spaces=[vmem, vmem, vmem, smem, smem],
        room=24,
    )
    pieces = total_everywhere(pieces)
    matrices = [pltpu.VMEM((total, total), F32), pltpu.VMEM((modes, total), F32)]
    cover, = call(
        functools.partial(cover_kernel, lon),
        [shape((modes * lon // LANES, LANES), F32)],
        pieces, high, low,
        flops=2 * 3 * modes * total * (total + wide),
        scratch=matrices,
    )

    def shifted(block, by):
        return lax.ppermute(block, "days", [(i, (i + by) % groups) for i in range(groups)])

    before, after = shifted(cover, 1), shifted(cover, 3)
    first, pcs, raw = call(
        first_kernel,
        [shape((modes, 2 * modes), F32), shape((modes, total), F32), shape((modes, total), F32)],
        pieces,
        flops=2 * 6 * modes * total * (total + 4 * modes),
        scratch=matrices,
    )
    before, after, first, pcs, raw = lax.optimization_barrier((before, after, first, pcs, raw))
    middle = cover.shape[0] // 2
    upper, lower = shifted(before[:middle], 1), shifted(after[middle:], 3)
    both, last = call(
        second_kernel,
        [shape((modes, 2 * modes), F32), shape((modes, total), F32)],
        first, pcs, raw,
        flops=2 * 6 * modes * total * (total + 4 * modes),
    )
    eofs, = call(
        patterns_kernel,
        [shape((modes, lat, lon), F32)],
        both, cover, before, after, upper, lower, where,
        flops=2 * 3 * modes * modes * lat * lon,
        spaces=[vmem] * 6 + [smem],
    )
    return (eofs, lax.dynamic_slice_in_dim(last, me * days, days, axis=1).T)


def solution(mesh):
    space = mesh.shape["space"]
    cores = 2
    around = 4 if space % 8 == 0 else 1
    parts = Mesh(
        mesh.devices.reshape(mesh.shape["days"], space // around // cores, around, cores),
        ("days", *SPACE),
    )
    placed = (
        P("days", SPACE, None), P("days"), P(SPACE), P(), P(None, SPACE, None),
    )
    return jax.shard_map(
        local,
        mesh=parts,
        in_specs=placed,
        out_specs=(P(None, SPACE, None), P("days", None)),
        check_vma=False,
    )
```

```python
import functools

import jax
import jax.numpy as jnp
from jax import lax
from jax.experimental import pallas as pl
from jax.experimental.pallas import tpu as pltpu
from jax.sharding import Mesh, PartitionSpec as P

LANES = 128
SIDE = 128
HIGH = lax.Precision.HIGHEST
F32 = jnp.float32
BF16 = jnp.bfloat16
INTERPRET = False
SPACE = ("z", "x", "core")
STAGES = ("core", ("days", "x"))
ALONG = "z"


def to_each(shard, axis):
    devices = lax.axis_size(axis)
    return lax.all_to_all(
        jnp.broadcast_to(shard[None], (devices, *shard.shape)), axis, 0, 0, tiled=True
    )


def dot(a, b, dims, precision=HIGH):
    return lax.dot_general(a, b, (dims, ((), ())), precision=precision, preferred_element_type=F32)


def one_pass(a, b, dims):
    return dot(a, b, dims, lax.Precision.DEFAULT)


NT = ((1,), (1,))
NN = ((1,), (0,))


def split(x):
    high = x.astype(BF16)
    return high, (x - high.astype(F32)).astype(BF16)


HALF = SIDE // 2
PANEL = 4


def lower_blocks(n):
    below, at = {}, 0
    for c in range(n):
        for r in range(c, n):
            below[r, c] = at
            at += SIDE if r > c else HALF
    return below, at


def positions(shape):
    return (lax.broadcasted_iota(jnp.int32, shape, 0), lax.broadcasted_iota(jnp.int32, shape, 1))


def folded(block):
    top, bottom = block[:HALF], block[HALF:]
    row, lane = positions(top.shape)
    rows = jnp.where(row > lane - HALF, jnp.where(lane < HALF, bottom, pltpu.roll(top, HALF, 1)), bottom)
    diagonal = jnp.sum(jnp.where(row == lane, top, 0.0), axis=0, keepdims=True)
    return rows, diagonal


def unfolded(rows, diagonal):
    row, lane = positions(rows.shape)
    top = jnp.where(lane < row, pltpu.roll(rows, HALF, 1), jnp.where(lane == row, diagonal, 0.0))
    bottom = jnp.where((lane < HALF) | (row <= lane - HALF), rows, 0.0)
    lower = jnp.concatenate([top, bottom], axis=0)
    row, lane = positions(lower.shape)
    return lower + jnp.where(row == lane, 0.0, lower).T


def sum_rows(n, modes):
    return lower_blocks(n)[1] + n * modes + 8


def payload_rows(days, lon):
    full, spare = divmod(lon, LANES)
    short = days * spare // LANES
    assert LANES % spare == 0 and short * LANES == days * spare and short % 8 == 0
    return full, spare, short, full * days + short + 8


def side_by_side(left, short):
    parts = left.shape[0] // short
    packed = left[:short]
    for g in range(1, parts):
        packed += pltpu.roll(left[g * short : (g + 1) * short], g * (LANES // parts), 1)
    return packed


def one_below_another(packed, parts):
    lane = lax.broadcasted_iota(jnp.int32, packed.shape, 1)
    width = LANES // parts
    pieces = [pltpu.roll(packed, LANES - g * width, 1) if g else packed for g in range(parts)]
    return jnp.concatenate([jnp.where(lane < width, piece, 0.0) for piece in pieces], axis=0)


def payload_kernel(fields_ref, label_ref, out_ref):
    lat, days, lon = fields_ref.shape
    full, spare, short, count = payload_rows(days, lon)
    label = label_ref[...].astype(F32)
    rest = jnp.zeros((1, LANES - (days - LANES)), F32)
    labels = jnp.concatenate(
        [label[:, :LANES], jnp.concatenate([label[:, LANES:], rest], axis=1), jnp.zeros((6, LANES), F32)]
    )
    for row in range(lat):
        for t in range(full):
            tile = fields_ref[row, :, t * LANES : (t + 1) * LANES].astype(F32)
            out_ref[row, t * days : (t + 1) * days] = tile
        left = fields_ref[row, :, full * LANES :].astype(F32)
        left = jnp.concatenate([left, jnp.zeros((days, LANES - spare), F32)], axis=1)
        out_ref[row, full * days : full * days + short] = side_by_side(left, short)
        out_ref[row, count - 8 :] = labels


def products_kernel(
    days, lon, rows_ref, base_ref, table_ref, row_ref, where_ref, core_ref,
    keep_ref, send_ref, high_ref, low_ref, out_ref,
):
    groups = rows_ref.shape[0]
    modes, wide = base_ref.shape
    full, spare, short, count = payload_rows(days, lon)
    total = groups * days
    n = total // SIDE

    def fields_of(d):
        tiles = [rows_ref[d, t * days : (t + 1) * days] for t in range(full)]
        packed = rows_ref[d, full * days : full * days + short]
        return jnp.concatenate(tiles + [one_below_another(packed, days // short)], axis=1)

    def hot_of(d):
        labels = rows_ref[d, count - 8 :]
        label = jnp.concatenate([labels[:1], labels[1:2]], axis=1)
        month = lax.broadcasted_iota(jnp.int32, (LANES, 2 * LANES), 0)
        day = lax.broadcasted_iota(jnp.int32, (LANES, 2 * LANES), 1)
        hit = ((month % 16).astype(F32) == label) & (month < 48) & (day < days)
        return jnp.where(hit, 1.0, 0.0)

    hots = [hot_of(d) for d in range(groups)]
    counts = sum(jnp.sum(hot[:16], axis=1, keepdims=True) for hot in hots)
    sums = sum(
        one_pass(hot[:16, :days].astype(BF16), fields_of(d).astype(BF16), NN)
        for d, hot in enumerate(hots)
    )
    climate = sums / jnp.maximum(counts, 1.0)
    first = climate.astype(BF16)
    rest = climate - first.astype(F32)
    second = rest.astype(BF16)
    third = (rest - second.astype(F32)).astype(BF16)
    terms = jnp.concatenate(
        [first.astype(F32), second.astype(F32), third.astype(F32), jnp.zeros((LANES - 48, wide), F32)]
    ).astype(BF16)
    entry = lax.broadcasted_iota(jnp.int32, table_ref.shape, 1)
    own = jnp.where(entry == row_ref[where_ref[0]], table_ref[...], 0.0)
    scale = jnp.sqrt(jnp.sum(own, axis=1, keepdims=True))
    for d in range(groups):
        part = slice(d * days, (d + 1) * days)
        hot = jnp.transpose(hots[d])[:days].astype(BF16)
        weighted = (fields_of(d) - one_pass(hot, terms, NN)) * scale
        high, low = split(weighted)
        high_ref[part] = high
        low_ref[part] = low
    days = total
    high_ref[days:] = base_ref[...]
    low_ref[days:] = jnp.zeros((modes, wide), BF16)
    below, end = lower_blocks(n)
    diagonals = []
    for c in range(0, n, 2):
        group = slice(c * SIDE, min(c + 2, n) * SIDE)
        under = slice(c * SIDE, days + modes)
        product = one_pass(high_ref[under], high_ref[group], NT)
        product += one_pass(high_ref[under], low_ref[group], NT)
        product += one_pass(low_ref[under], high_ref[group], NT)
        for k in range(c, min(c + 2, n)):
            lanes = slice((k - c) * SIDE, (k - c + 1) * SIDE)
            for r in range(k, n):
                at = below[r, k]
                block = product[(r - c) * SIDE : (r - c + 1) * SIDE, lanes]
                if r > k:
                    out_ref[at : at + SIDE] = block
                else:
                    out_ref[at : at + HALF], diagonal = folded(block)
                    diagonals.append(diagonal)
            at = end + k * modes
            out_ref[at : at + modes] = product[days - c * SIDE :, lanes]
    at = end + n * modes
    out_ref[at : at + 8] = jnp.concatenate(diagonals + [jnp.zeros((8 - n, LANES), F32)], axis=0)
    at += 8
    if at < out_ref.shape[0]:
        out_ref[at:] = jnp.zeros((out_ref.shape[0] - at, LANES), F32)
    keep_ref[...], send_ref[...] = in_order(out_ref[: count_of(out_ref)], out_ref[count_of(out_ref) :], core_ref)


def count_of(rows_ref):
    return rows_ref.shape[0] // 2


def in_order(mine, other, core_ref):
    first = core_ref[0] == 0
    return jnp.where(first, mine, other), jnp.where(first, other, mine)


def add_kernel(keep_ref, other_ref, out_ref):
    out_ref[...] = keep_ref[...] + other_ref[...]


def assemble(mine_ref, other_ref, core_ref, rows_ref, products_ref, pcs_ref):
    half = count_of(rows_ref)
    rows_ref[:half], rows_ref[half:] = in_order(mine_ref[...], other_ref[...], core_ref)
    modes, days = pcs_ref.shape
    n = days // SIDE
    below, end = lower_blocks(n)
    diagonals = rows_ref[end + n * modes : end + n * modes + 8]
    for (r, c), at in below.items():
        rows, lanes = slice(r * SIDE, (r + 1) * SIDE), slice(c * SIDE, (c + 1) * SIDE)
        if r > c:
            block = rows_ref[at : at + SIDE] * (1.0 / days)
            products_ref[rows, lanes] = block
            products_ref[lanes, rows] = block.T
        else:
            block = unfolded(rows_ref[at : at + HALF], diagonals[r : r + 1])
            products_ref[rows, lanes] = block * (1.0 / days)
    for i in range(n):
        at = end + i * modes
        pcs_ref[:, i * SIDE : (i + 1) * SIDE] = rows_ref[at : at + modes]


def cover_kernel(
    lon, mine_ref, other_ref, high_ref, low_ref, core_ref, cover_ref, rows_ref, products_ref, pcs_ref
):
    modes, days = pcs_ref.shape
    assemble(mine_ref, other_ref, core_ref, rows_ref, products_ref, pcs_ref)
    raw = dot(pcs_ref[...], products_ref[...], NN)
    high, low = split(raw * (1.0 / days))
    both = jnp.concatenate([high, low], axis=0)
    by_high = one_pass(both, high_ref[:days], NN)
    by_low = one_pass(high, low_ref[:days], NN)
    cover = by_high[:modes] + by_high[modes:] + by_low
    full, _, short, _ = payload_rows(modes, lon)
    for t in range(full):
        cover_ref[t * modes : (t + 1) * modes] = cover[:, t * LANES : (t + 1) * LANES]
    cover_ref[full * modes :] = side_by_side(cover[:, full * LANES :], short)


def inverse_factor(gram, modes):
    row = lax.broadcasted_iota(jnp.int32, gram.shape, 0)
    lane = lax.broadcasted_iota(jnp.int32, gram.shape, 1)
    whole = jnp.where(lane < modes, jnp.where(row == lane, 1.0, 0.0), gram)
    blocks = [whole[at : at + 8] for at in range(0, modes, 8)]
    full = (8, gram.shape[1])
    sub = lax.broadcasted_iota(jnp.int32, full, 0)
    for start in range(0, modes, PANEL):
        own, at = divmod(start, 8)
        spots = range(modes + start, modes + start + PANEL)
        rows = [jnp.broadcast_to(blocks[own][at + i : at + i + 1], full) for i in range(PANEL)]
        entry = [
            [jnp.broadcast_to(blocks[own][at + i : at + i + 1, spot : spot + 1], full) for spot in spots]
            for i in range(PANEL)
        ]
        factor = [[None] * PANEL for _ in range(PANEL)]
        scaled = []
        for k in range(PANEL):
            inverse = 1.0 / entry[k][k]
            for i in range(k + 1, PANEL):
                factor[i][k] = entry[i][k] * inverse
            for i in range(k + 1, PANEL):
                for m in range(k + 1, i + 1):
                    entry[i][m] = entry[i][m] - factor[i][k] * entry[m][k]
                rows[i] = rows[i] - factor[i][k] * rows[k]
            scaled.append(rows[k] * inverse)
        for b in range(own, modes // 8):
            columns = []
            step = None
            for k, spot in enumerate(spots):
                column = jnp.broadcast_to(blocks[b][:, spot : spot + 1], full)
                for m in range(k):
                    column = column - columns[m] * factor[k][m]
                columns.append(column)
                if b == own:
                    column = jnp.where(sub > at + k, column, 0.0)
                step = column * scaled[k] if step is None else step + column * scaled[k]
            blocks[b] = blocks[b] - step
    whole = jnp.concatenate(blocks, axis=0)
    pivots = jnp.sum(jnp.where(lane == row + modes, whole, 0.0), axis=1, keepdims=True)
    return jnp.where(lane < modes, whole / jnp.sqrt(pivots), 0.0)


def first_kernel(
    mine_ref, other_ref, core_ref, first_ref, new_pcs_ref, raw_ref, rows_ref, products_ref, pcs_ref
):
    modes, days = pcs_ref.shape
    assemble(mine_ref, other_ref, core_ref, rows_ref, products_ref, pcs_ref)
    nothing = jnp.zeros((modes, days), F32)
    raw = dot(pcs_ref[...], products_ref[...], NN)
    gram = dot(pcs_ref[...], jnp.concatenate([nothing, raw]), NT) * (1.0 / days)
    first = inverse_factor(gram, modes)
    pcs = dot(first, jnp.concatenate([raw, nothing]), NN)
    first_ref[...] = first
    new_pcs_ref[...] = pcs
    raw_ref[...] = dot(pcs, products_ref[...], NN)


def second_kernel(first_ref, pcs_ref, raw_ref, where_ref, both_ref, last_ref):
    modes, days = pcs_ref.shape
    nothing = jnp.zeros((modes, days), F32)
    raw = raw_ref[...]
    gram = dot(pcs_ref[...], jnp.concatenate([nothing, raw]), NT) * (1.0 / days)
    second = inverse_factor(gram, modes)
    first = first_ref[...]
    last = dot(second, jnp.concatenate([raw, nothing]), NN)
    own = last_ref.shape[1]
    last_ref[...] = last[:, :own]
    for part in range(1, days // own):
        @pl.when(where_ref[0] == part)
        def _():
            last_ref[...] = last[:, part * own : (part + 1) * own]
    both_ref[...] = dot(second, jnp.concatenate([first, jnp.zeros_like(first)]), NN)


def patterns_kernel(both_ref, own_ref, before_ref, after_ref, upper_ref, lower_ref, where_ref, out_ref):
    modes, lat, lon = out_ref.shape
    me = where_ref[0]
    full, _, short, _ = payload_rows(modes, lon)
    high, low = split(both_ref[:, :modes])
    stacked = jnp.concatenate([high, low], axis=0)
    across = jnp.concatenate([upper_ref[...], lower_ref[...]], axis=0)
    for row in range(lat):
        ahead = lax.rem(row - me + lat, lat)
        cover = jnp.where(
            ahead == 0,
            own_ref[...],
            jnp.where(ahead == 1, after_ref[...], jnp.where(ahead == 2, across, before_ref[...])),
        )
        tiles = [cover[t * modes : (t + 1) * modes] for t in range(full)]
        tiles.append(one_below_another(cover[full * modes :], modes // short))
        cover_high, cover_low = split(jnp.concatenate(tiles, axis=1))
        by_high = one_pass(stacked, cover_high, NN)
        rows = by_high[:modes] + by_high[modes:] + one_pass(high, cover_low, NN)
        out_ref[:, row, :] = rows[:, :lon]


def call(kernel, shapes, *arrays, flops, spaces=None, scratch=(), room=16):
    whole = pl.BlockSpec(memory_space=pltpu.VMEM)
    size = sum(a.size * a.dtype.itemsize for a in arrays)
    size += sum(a.size * a.dtype.itemsize for a in shapes)
    return pl.pallas_call(
        kernel,
        out_shape=shapes,
        in_specs=spaces or [whole] * len(arrays),
        out_specs=[whole] * len(shapes),
        scratch_shapes=scratch,
        cost_estimate=pl.CostEstimate(flops=flops, bytes_accessed=size, transcendentals=0),
        compiler_params=pltpu.CompilerParams(vmem_limit_bytes=room * 2**20),
        interpret=INTERPRET,
    )(*arrays)


def sum_kernel(tiles_ref, out_ref):
    out_ref[...] = jnp.broadcast_to(jnp.sum(tiles_ref[...], axis=0), out_ref.shape)


def summed(tiles, copies=0):
    tail = tiles.shape[1:]
    out, = call(
        sum_kernel,
        [jax.ShapeDtypeStruct((copies, *tail) if copies else tail, F32)],
        tiles,
        flops=tiles.size,
        room=8,
    )
    return out


def swapped(rows, axis):
    return lax.ppermute(rows, axis, [(0, 1), (1, 0)])


def total_everywhere(keep, send):
    def exchanged(tiles, axis):
        return lax.all_to_all(tiles, axis, 0, 0, tiled=True)

    near, plane = STAGES
    rows, = call(add_kernel, [jax.ShapeDtypeStruct(keep.shape, F32)], keep, swapped(send, near), flops=keep.size, room=8)
    tiles = exchanged(rows.reshape(lax.axis_size(plane), -1, LANES), plane)
    tiles = exchanged(summed(tiles, lax.axis_size(ALONG)), ALONG)
    rows = exchanged(summed(tiles, lax.axis_size(plane)), plane).reshape(-1, LANES)
    return rows, swapped(rows, near)


def local(fields, month_label, row_index, area_table, basis):
    days, lat, lon = fields.shape
    groups = lax.axis_size("days")
    me = lax.axis_index("days")
    wide = -(-(lon + 1) // LANES) * LANES
    modes = basis.shape[0]
    total = days * groups
    n = total // SIDE
    shape = jax.ShapeDtypeStruct

    fields, after_it = lax.optimization_barrier((jnp.swapaxes(fields, 0, 1), me))
    rows, = call(
        payload_kernel,
        [shape((lat, payload_rows(days, lon)[-1], LANES), F32)],
        fields, month_label.reshape(1, -1),
        flops=fields.size,
    )
    start = lax.dynamic_index_in_dim(basis, after_it, axis=1, keepdims=False)
    start = jnp.pad(start, ((0, 0), (0, wide - lon)))
    where = me.astype(jnp.int32).reshape(1)
    core = lax.axis_index("core").astype(jnp.int32).reshape(1)
    rows, start, where, core = lax.optimization_barrier((rows, start, where, core))
    rows = lax.all_to_all(rows, "days", 0, 0, tiled=True)

    count = sum_rows(n, modes)
    devices = groups * lax.axis_size(SPACE)
    count += -count % devices
    vmem, smem = pl.BlockSpec(memory_space=pltpu.VMEM), pl.BlockSpec(memory_space=pltpu.SMEM)
    tall = total + modes
    half = shape((count // 2, LANES), F32)
    keep, send, high, low = call(
        functools.partial(products_kernel, days, lon),
        [half, half, shape((tall, wide), BF16), shape((tall, wide), BF16)],
        rows, start, area_table.reshape(1, -1), row_index, where, core,
        flops=2 * 3 * total * tall * wide,
        spaces=[vmem, vmem, vmem, smem, smem, smem],
        scratch=[pltpu.VMEM((count, LANES), F32)],
        room=24,
    )
    mine, other = total_everywhere(keep, send)
    matrices = [pltpu.VMEM((count, LANES), F32), pltpu.VMEM((total, total), F32), pltpu.VMEM((modes, total), F32)]
    cover, = call(
        functools.partial(cover_kernel, lon),
        [shape((modes * lon // LANES, LANES), F32)],
        mine, other, high, low, core,
        flops=2 * 3 * modes * total * (total + wide),
        spaces=[vmem] * 4 + [smem],
        scratch=matrices,
    )

    def shifted(block, by):
        return lax.ppermute(block, "days", [(i, (i + by) % groups) for i in range(groups)])

    before, after = shifted(cover, 1), shifted(cover, 3)
    first, pcs, raw = call(
        first_kernel,
        [shape((modes, 2 * modes), F32), shape((modes, total), F32), shape((modes, total), F32)],
        mine, other, core,
        flops=2 * 6 * modes * total * (total + 4 * modes),
        spaces=[vmem, vmem, smem],
        scratch=matrices,
    )
    before, after, first, pcs, raw = lax.optimization_barrier((before, after, first, pcs, raw))
    middle = cover.shape[0] // 2
    upper, lower = shifted(before[:middle], 1), shifted(after[middle:], 3)
    both, last = call(
        second_kernel,
        [shape((modes, 2 * modes), F32), shape((modes, days), F32)],
        first, pcs, raw, where,
        flops=2 * 6 * modes * total * (total + 4 * modes),
        spaces=[vmem] * 3 + [smem],
    )
    eofs, = call(
        patterns_kernel,
        [shape((modes, lat, lon), F32)],
        both, cover, before, after, upper, lower, where,
        flops=2 * 3 * modes * modes * lat * lon,
        spaces=[vmem] * 6 + [smem],
    )
    return (eofs, last.T)


def solution(mesh):
    space = mesh.shape["space"]
    cores = 2
    around = 4 if space % 8 == 0 else 1
    parts = Mesh(
        mesh.devices.reshape(mesh.shape["days"], space // around // cores, around, cores),
        ("days", *SPACE),
    )
    placed = (
        P("days", SPACE, None), P("days"), P(SPACE), P(), P(None, SPACE, None),
    )
    return jax.shard_map(
        local,
        mesh=parts,
        in_specs=placed,
        out_specs=(P(None, SPACE, None), P("days", None)),
        check_vma=False,
    )
```

```python
import functools

import jax
import jax.numpy as jnp
from jax import lax
from jax.experimental import pallas as pl
from jax.experimental.pallas import tpu as pltpu
from jax.sharding import Mesh, PartitionSpec as P

LANES = 128
SIDE = 128
HIGH = lax.Precision.HIGHEST
F32 = jnp.float32
BF16 = jnp.bfloat16
INTERPRET = False
SPACE = ("z", "x", "core")
STAGES = ("core", ("days", "x"))
ALONG = "z"


def to_each(shard, axis):
    devices = lax.axis_size(axis)
    return lax.all_to_all(
        jnp.broadcast_to(shard[None], (devices, *shard.shape)), axis, 0, 0, tiled=True
    )


def dot(a, b, dims, precision=HIGH):
    return lax.dot_general(a, b, (dims, ((), ())), precision=precision, preferred_element_type=F32)


def one_pass(a, b, dims):
    return dot(a, b, dims, lax.Precision.DEFAULT)


NT = ((1,), (1,))
NN = ((1,), (0,))


def split(x):
    high = x.astype(BF16)
    return high, (x - high.astype(F32)).astype(BF16)


HALF = SIDE // 2
PANEL = 4


def lower_blocks(n):
    below, at = {}, 0
    for c in range(n):
        for r in range(c, n):
            below[r, c] = at
            at += SIDE if r > c else HALF
    return below, at


def positions(shape):
    return (lax.broadcasted_iota(jnp.int32, shape, 0), lax.broadcasted_iota(jnp.int32, shape, 1))


def folded(block):
    top, bottom = block[:HALF], block[HALF:]
    row, lane = positions(top.shape)
    rows = jnp.where(row > lane - HALF, jnp.where(lane < HALF, bottom, pltpu.roll(top, HALF, 1)), bottom)
    diagonal = jnp.sum(jnp.where(row == lane, top, 0.0), axis=0, keepdims=True)
    return rows, diagonal


def unfolded(rows, diagonal):
    row, lane = positions(rows.shape)
    top = jnp.where(lane < row, pltpu.roll(rows, HALF, 1), jnp.where(lane == row, diagonal, 0.0))
    bottom = jnp.where((lane < HALF) | (row <= lane - HALF), rows, 0.0)
    lower = jnp.concatenate([top, bottom], axis=0)
    row, lane = positions(lower.shape)
    return lower + jnp.where(row == lane, 0.0, lower).T


def sum_rows(n, modes):
    return lower_blocks(n)[1] + n * modes + 8


def payload_rows(days, lon):
    full, spare = divmod(lon, LANES)
    short = days * spare // LANES
    assert LANES % spare == 0 and short * LANES == days * spare and short % 8 == 0
    return full, spare, short, full * days + short + 8


def side_by_side(left, short):
    parts = left.shape[0] // short
    packed = left[:short]
    for g in range(1, parts):
        packed += pltpu.roll(left[g * short : (g + 1) * short], g * (LANES // parts), 1)
    return packed


def one_below_another(packed, parts):
    lane = lax.broadcasted_iota(jnp.int32, packed.shape, 1)
    width = LANES // parts
    pieces = [pltpu.roll(packed, LANES - g * width, 1) if g else packed for g in range(parts)]
    return jnp.concatenate([jnp.where(lane < width, piece, 0.0) for piece in pieces], axis=0)


def payload_kernel(fields_ref, label_ref, out_ref):
    lat, days, lon = fields_ref.shape
    full, spare, short, count = payload_rows(days, lon)
    label = label_ref[...].astype(F32)
    rest = jnp.zeros((1, LANES - (days - LANES)), F32)
    labels = jnp.concatenate(
        [label[:, :LANES], jnp.concatenate([label[:, LANES:], rest], axis=1), jnp.zeros((6, LANES), F32)]
    )
    for row in range(lat):
        for t in range(full):
            tile = fields_ref[row, :, t * LANES : (t + 1) * LANES].astype(F32)
            out_ref[row, t * days : (t + 1) * days] = tile
        left = fields_ref[row, :, full * LANES :].astype(F32)
        left = jnp.concatenate([left, jnp.zeros((days, LANES - spare), F32)], axis=1)
        out_ref[row, full * days : full * days + short] = side_by_side(left, short)
        out_ref[row, count - 8 :] = labels


def products_kernel(
    days, lon, rows_ref, base_ref, table_ref, row_ref, where_ref, core_ref,
    keep_ref, send_ref, high_ref, low_ref, out_ref,
):
    groups = rows_ref.shape[0]
    modes, wide = base_ref.shape
    full, spare, short, count = payload_rows(days, lon)
    total = groups * days
    n = total // SIDE

    def fields_of(d):
        tiles = [rows_ref[d, t * days : (t + 1) * days] for t in range(full)]
        packed = rows_ref[d, full * days : full * days + short]
        return jnp.concatenate(tiles + [one_below_another(packed, days // short)], axis=1)

    def hot_of(d):
        labels = rows_ref[d, count - 8 :]
        label = jnp.concatenate([labels[:1], labels[1:2]], axis=1)
        month = lax.broadcasted_iota(jnp.int32, (LANES, 2 * LANES), 0)
        day = lax.broadcasted_iota(jnp.int32, (LANES, 2 * LANES), 1)
        hit = ((month % 16).astype(F32) == label) & (month < 48) & (day < days)
        return jnp.where(hit, 1.0, 0.0)

    hots = [hot_of(d) for d in range(groups)]
    counts = sum(jnp.sum(hot[:16], axis=1, keepdims=True) for hot in hots)
    sums = sum(
        one_pass(hot[:16, :days].astype(BF16), fields_of(d).astype(BF16), NN)
        for d, hot in enumerate(hots)
    )
    climate = sums / jnp.maximum(counts, 1.0)
    first = climate.astype(BF16)
    rest = climate - first.astype(F32)
    second = rest.astype(BF16)
    third = (rest - second.astype(F32)).astype(BF16)
    terms = jnp.concatenate(
        [first.astype(F32), second.astype(F32), third.astype(F32), jnp.zeros((LANES - 48, wide), F32)]
    ).astype(BF16)
    entry = lax.broadcasted_iota(jnp.int32, table_ref.shape, 1)
    own = jnp.where(entry == row_ref[where_ref[0]], table_ref[...], 0.0)
    scale = jnp.sqrt(jnp.sum(own, axis=1, keepdims=True))
    for d in range(groups):
        part = slice(d * days, (d + 1) * days)
        hot = jnp.transpose(hots[d])[:days].astype(BF16)
        weighted = (fields_of(d) - one_pass(hot, terms, NN)) * scale
        high, low = split(weighted)
        high_ref[part] = high
        low_ref[part] = low
    days = total
    high_ref[days:] = base_ref[...]
    low_ref[days:] = jnp.zeros((modes, wide), BF16)
    below, end = lower_blocks(n)
    diagonals = []
    for c in range(0, n, 2):
        group = slice(c * SIDE, min(c + 2, n) * SIDE)
        under = slice(c * SIDE, days + modes)
        product = one_pass(high_ref[under], high_ref[group], NT)
        product += one_pass(high_ref[under], low_ref[group], NT)
        product += one_pass(low_ref[under], high_ref[group], NT)
        for k in range(c, min(c + 2, n)):
            lanes = slice((k - c) * SIDE, (k - c + 1) * SIDE)
            for r in range(k, n):
                at = below[r, k]
                block = product[(r - c) * SIDE : (r - c + 1) * SIDE, lanes]
                if r > k:
                    out_ref[at : at + SIDE] = block
                else:
                    out_ref[at : at + HALF], diagonal = folded(block)
                    diagonals.append(diagonal)
            at = end + k * modes
            out_ref[at : at + modes] = product[days - c * SIDE :, lanes]
    at = end + n * modes
    out_ref[at : at + 8] = jnp.concatenate(diagonals + [jnp.zeros((8 - n, LANES), F32)], axis=0)
    at += 8
    if at < out_ref.shape[0]:
        out_ref[at:] = jnp.zeros((out_ref.shape[0] - at, LANES), F32)
    keep_ref[...], send_ref[...] = in_order(out_ref[: count_of(out_ref)], out_ref[count_of(out_ref) :], core_ref)


def count_of(rows_ref):
    return rows_ref.shape[0] // 2


def in_order(mine, other, core_ref):
    first = core_ref[0] == 0
    return jnp.where(first, mine, other), jnp.where(first, other, mine)


def add_kernel(keep_ref, other_ref, out_ref):
    out_ref[...] = keep_ref[...] + other_ref[...]


def assemble(mine_ref, other_ref, core_ref, rows_ref, products_ref, pcs_ref):
    half = count_of(rows_ref)
    rows_ref[:half], rows_ref[half:] = in_order(mine_ref[...], other_ref[...], core_ref)
    modes, days = pcs_ref.shape
    n = days // SIDE
    below, end = lower_blocks(n)
    diagonals = rows_ref[end + n * modes : end + n * modes + 8]
    for (r, c), at in below.items():
        rows, lanes = slice(r * SIDE, (r + 1) * SIDE), slice(c * SIDE, (c + 1) * SIDE)
        if r > c:
            block = rows_ref[at : at + SIDE] * (1.0 / days)
            products_ref[rows, lanes] = block
            products_ref[lanes, rows] = block.T
        else:
            block = unfolded(rows_ref[at : at + HALF], diagonals[r : r + 1])
            products_ref[rows, lanes] = block * (1.0 / days)
    for i in range(n):
        at = end + i * modes
        pcs_ref[:, i * SIDE : (i + 1) * SIDE] = rows_ref[at : at + modes]


def cover_kernel(
    lon, mine_ref, other_ref, high_ref, low_ref, core_ref, upper_ref, lower_ref,
    rows_ref, products_ref, pcs_ref,
):
    modes, days = pcs_ref.shape
    assemble(mine_ref, other_ref, core_ref, rows_ref, products_ref, pcs_ref)
    raw = dot(pcs_ref[...], products_ref[...], NN)
    high, low = split(raw * (1.0 / days))
    both = jnp.concatenate([high, low], axis=0)
    by_high = one_pass(both, high_ref[:days], NN)
    by_low = one_pass(high, low_ref[:days], NN)
    cover = by_high[:modes] + by_high[modes:] + by_low
    full, _, short, _ = payload_rows(modes, lon)
    rows = [cover[:, t * LANES : (t + 1) * LANES] for t in range(full)]
    rows = jnp.concatenate(rows + [side_by_side(cover[:, full * LANES :], short)], axis=0)
    upper_ref[...] = rows[: upper_ref.shape[0]]
    lower_ref[...] = rows[upper_ref.shape[0] :]


def inverse_factor(gram, modes):
    row = lax.broadcasted_iota(jnp.int32, gram.shape, 0)
    lane = lax.broadcasted_iota(jnp.int32, gram.shape, 1)
    whole = jnp.where(lane < modes, jnp.where(row == lane, 1.0, 0.0), gram)
    blocks = [whole[at : at + 8] for at in range(0, modes, 8)]
    full = (8, gram.shape[1])
    sub = lax.broadcasted_iota(jnp.int32, full, 0)
    for start in range(0, modes, PANEL):
        own, at = divmod(start, 8)
        spots = range(modes + start, modes + start + PANEL)
        rows = [jnp.broadcast_to(blocks[own][at + i : at + i + 1], full) for i in range(PANEL)]
        entry = [
            [jnp.broadcast_to(blocks[own][at + i : at + i + 1, spot : spot + 1], full) for spot in spots]
            for i in range(PANEL)
        ]
        factor = [[None] * PANEL for _ in range(PANEL)]
        scaled = []
        for k in range(PANEL):
            inverse = 1.0 / entry[k][k]
            for i in range(k + 1, PANEL):
                factor[i][k] = entry[i][k] * inverse
            for i in range(k + 1, PANEL):
                for m in range(k + 1, i + 1):
                    entry[i][m] = entry[i][m] - factor[i][k] * entry[m][k]
                rows[i] = rows[i] - factor[i][k] * rows[k]
            scaled.append(rows[k] * inverse)
        for b in range(own, modes // 8):
            columns = []
            step = None
            for k, spot in enumerate(spots):
                column = jnp.broadcast_to(blocks[b][:, spot : spot + 1], full)
                for m in range(k):
                    column = column - columns[m] * factor[k][m]
                columns.append(column)
                if b == own:
                    column = jnp.where(sub > at + k, column, 0.0)
                step = column * scaled[k] if step is None else step + column * scaled[k]
            blocks[b] = blocks[b] - step
    whole = jnp.concatenate(blocks, axis=0)
    pivots = jnp.sum(jnp.where(lane == row + modes, whole, 0.0), axis=1, keepdims=True)
    return jnp.where(lane < modes, whole / jnp.sqrt(pivots), 0.0)


def first_kernel(
    mine_ref, other_ref, core_ref, first_ref, new_pcs_ref, raw_ref, rows_ref, products_ref, pcs_ref
):
    modes, days = pcs_ref.shape
    assemble(mine_ref, other_ref, core_ref, rows_ref, products_ref, pcs_ref)
    nothing = jnp.zeros((modes, days), F32)
    raw = dot(pcs_ref[...], products_ref[...], NN)
    gram = dot(pcs_ref[...], jnp.concatenate([nothing, raw]), NT) * (1.0 / days)
    first = inverse_factor(gram, modes)
    pcs = dot(first, jnp.concatenate([raw, nothing]), NN)
    first_ref[...] = first
    new_pcs_ref[...] = pcs
    raw_ref[...] = dot(pcs, products_ref[...], NN)


def second_kernel(first_ref, pcs_ref, raw_ref, where_ref, both_ref, last_ref):
    modes, days = pcs_ref.shape
    nothing = jnp.zeros((modes, days), F32)
    raw = raw_ref[...]
    gram = dot(pcs_ref[...], jnp.concatenate([nothing, raw]), NT) * (1.0 / days)
    second = inverse_factor(gram, modes)
    first = first_ref[...]
    last = dot(second, jnp.concatenate([raw, nothing]), NN)
    own = last_ref.shape[1]
    last_ref[...] = last[:, :own]
    for part in range(1, days // own):
        @pl.when(where_ref[0] == part)
        def _():
            last_ref[...] = last[:, part * own : (part + 1) * own]
    both_ref[...] = dot(second, jnp.concatenate([first, jnp.zeros_like(first)]), NN)


def patterns_kernel(both_ref, *refs):
    *cover_refs, where_ref, out_ref = refs
    modes, lat, lon = out_ref.shape
    me = where_ref[0]
    own, before, after, across = [
        jnp.concatenate([cover_refs[i][...], cover_refs[i + 1][...]], axis=0) for i in (0, 2, 4, 6)
    ]
    full, _, short, _ = payload_rows(modes, lon)
    high, low = split(both_ref[:, :modes])
    stacked = jnp.concatenate([high, low], axis=0)
    for row in range(lat):
        ahead = lax.rem(row - me + lat, lat)
        cover = jnp.where(
            ahead == 0,
            own,
            jnp.where(ahead == 1, after, jnp.where(ahead == 2, across, before)),
        )
        tiles = [cover[t * modes : (t + 1) * modes] for t in range(full)]
        tiles.append(one_below_another(cover[full * modes :], modes // short))
        cover_high, cover_low = split(jnp.concatenate(tiles, axis=1))
        by_high = one_pass(stacked, cover_high, NN)
        rows = by_high[:modes] + by_high[modes:] + one_pass(high, cover_low, NN)
        out_ref[:, row, :] = rows[:, :lon]


def call(kernel, shapes, *arrays, flops, spaces=None, scratch=(), room=16):
    whole = pl.BlockSpec(memory_space=pltpu.VMEM)
    size = sum(a.size * a.dtype.itemsize for a in arrays)
    size += sum(a.size * a.dtype.itemsize for a in shapes)
    return pl.pallas_call(
        kernel,
        out_shape=shapes,
        in_specs=spaces or [whole] * len(arrays),
        out_specs=[whole] * len(shapes),
        scratch_shapes=scratch,
        cost_estimate=pl.CostEstimate(flops=flops, bytes_accessed=size, transcendentals=0),
        compiler_params=pltpu.CompilerParams(vmem_limit_bytes=room * 2**20),
        interpret=INTERPRET,
    )(*arrays)


def sum_kernel(tiles_ref, out_ref):
    out_ref[...] = jnp.broadcast_to(jnp.sum(tiles_ref[...], axis=0), out_ref.shape)


def summed(tiles, copies=0):
    tail = tiles.shape[1:]
    out, = call(
        sum_kernel,
        [jax.ShapeDtypeStruct((copies, *tail) if copies else tail, F32)],
        tiles,
        flops=tiles.size,
        room=8,
    )
    return out


def swapped(rows, axis):
    return lax.ppermute(rows, axis, [(0, 1), (1, 0)])


def total_everywhere(keep, send):
    def exchanged(tiles, axis):
        return lax.all_to_all(tiles, axis, 0, 0, tiled=True)

    near, plane = STAGES
    rows, = call(add_kernel, [jax.ShapeDtypeStruct(keep.shape, F32)], keep, swapped(send, near), flops=keep.size, room=8)
    tiles = exchanged(rows.reshape(lax.axis_size(plane), -1, LANES), plane)
    tiles = exchanged(summed(tiles, lax.axis_size(ALONG)), ALONG)
    rows = exchanged(summed(tiles, lax.axis_size(plane)), plane).reshape(-1, LANES)
    return rows, swapped(rows, near)


def local(fields, month_label, row_index, area_table, basis):
    days, lat, lon = fields.shape
    groups = lax.axis_size("days")
    me = lax.axis_index("days")
    wide = -(-(lon + 1) // LANES) * LANES
    modes = basis.shape[0]
    total = days * groups
    n = total // SIDE
    shape = jax.ShapeDtypeStruct

    fields, after_it = lax.optimization_barrier((jnp.swapaxes(fields, 0, 1), me))
    rows, = call(
        payload_kernel,
        [shape((lat, payload_rows(days, lon)[-1], LANES), F32)],
        fields, month_label.reshape(1, -1),
        flops=fields.size,
    )
    start = lax.dynamic_index_in_dim(basis, after_it, axis=1, keepdims=False)
    start = jnp.pad(start, ((0, 0), (0, wide - lon)))
    where = me.astype(jnp.int32).reshape(1)
    core = lax.axis_index("core").astype(jnp.int32).reshape(1)
    rows, start, where, core = lax.optimization_barrier((rows, start, where, core))
    rows = lax.all_to_all(rows, "days", 0, 0, tiled=True)

    count = sum_rows(n, modes)
    devices = groups * lax.axis_size(SPACE)
    count += -count % devices
    vmem, smem = pl.BlockSpec(memory_space=pltpu.VMEM), pl.BlockSpec(memory_space=pltpu.SMEM)
    tall = total + modes
    half = shape((count // 2, LANES), F32)
    keep, send, high, low = call(
        functools.partial(products_kernel, days, lon),
        [half, half, shape((tall, wide), BF16), shape((tall, wide), BF16)],
        rows, start, area_table.reshape(1, -1), row_index, where, core,
        flops=2 * 3 * total * tall * wide,
        spaces=[vmem, vmem, vmem, smem, smem, smem],
        scratch=[pltpu.VMEM((count, LANES), F32)],
        room=24,
    )
    mine, other = total_everywhere(keep, send)
    matrices = [pltpu.VMEM((count, LANES), F32), pltpu.VMEM((total, total), F32), pltpu.VMEM((modes, total), F32)]
    piece = shape((modes * lon // LANES // 2, LANES), F32)
    own_upper, own_lower = call(
        functools.partial(cover_kernel, lon),
        [piece, piece],
        mine, other, high, low, core,
        flops=2 * 3 * modes * total * (total + wide),
        spaces=[vmem] * 4 + [smem],
        scratch=matrices,
    )

    def shifted(block, by):
        return lax.ppermute(block, "days", [(i, (i + by) % groups) for i in range(groups)])

    before_upper, after_lower = shifted(own_upper, 1), shifted(own_lower, 3)
    before_lower, after_upper = shifted(own_lower, 1), shifted(own_upper, 3)
    first, pcs, raw = call(
        first_kernel,
        [shape((modes, 2 * modes), F32), shape((modes, total), F32), shape((modes, total), F32)],
        mine, other, core,
        flops=2 * 6 * modes * total * (total + 4 * modes),
        spaces=[vmem, vmem, smem],
        scratch=matrices,
    )
    before_upper, after_lower, first, pcs, raw = lax.optimization_barrier(
        (before_upper, after_lower, first, pcs, raw)
    )
    across_upper, across_lower = shifted(before_upper, 1), shifted(after_lower, 3)
    both, last = call(
        second_kernel,
        [shape((modes, 2 * modes), F32), shape((modes, days), F32)],
        first, pcs, raw, where,
        flops=2 * 6 * modes * total * (total + 4 * modes),
        spaces=[vmem] * 3 + [smem],
    )
    eofs, = call(
        patterns_kernel,
        [shape((modes, lat, lon), F32)],
        both, own_upper, own_lower, before_upper, before_lower, after_upper, after_lower,
        across_upper, across_lower, where,
        flops=2 * 3 * modes * modes * lat * lon,
        spaces=[vmem] * 9 + [smem],
    )
    return (eofs, last.T)


def solution(mesh):
    space = mesh.shape["space"]
    cores = 2
    around = 4 if space % 8 == 0 else 1
    parts = Mesh(
        mesh.devices.reshape(mesh.shape["days"], space // around // cores, around, cores),
        ("days", *SPACE),
    )
    placed = (
        P("days", SPACE, None), P("days"), P(SPACE), P(), P(None, SPACE, None),
    )
    return jax.shard_map(
        local,
        mesh=parts,
        in_specs=placed,
        out_specs=(P(None, SPACE, None), P("days", None)),
        check_vma=False,
    )
```
